256 devices in a mesh: seq: 32 (over z, x_hi, core), tp: 8 (over x_lo, y).
Axes of the slice: x: 4 (x_hi: 2, x_lo: 2; x = x_hi * 2 + x_lo), y: 4, z: 8, core: 2. Of those that a mesh axis runs over, the one named last changes fastest.
Arguments:
- tokens: bfloat16 [8192, 2048], P('seq', 'tp'), may hold values from -6 to 6
- ctx_len: int32 [32], P('seq'), may hold values from 0 to 12288, as said below
- cache_kv: bfloat16 [32, 4096, 2, 2048], P('seq', None, None, 'tp'), may hold values from -80 to 80, as said below
- cache_pos: int32 [32, 4096], P('seq'), may hold values from -1 to 12287, as said below
- attn_gain: float32 [2048], replicated, may hold values from 0.5 to 1.5
- moe_gain: float32 [2048], replicated, may hold values from 0.5 to 1.5
- qkv_train: float32 [2048, 3, 2048], P('seq', None, 'tp'), may hold values from -0.125 to 0.125
- out_train: float32 [2048, 2048], P('seq', 'tp'), may hold values from -0.125 to 0.125
- router: bfloat16 [2048, 64], replicated, may hold values from -0.125 to 0.125
- routes: int32 [8192, 6], P('seq'), may hold values from 0 to 63, all different within a row; in each aligned block of 256 rows (0 to 255, 256 to 511, ...) at most 32 rows name the same one
- handed_half: int32 [32], replicated, may hold values from 0 to 1
- fresh_gu: float32 [32, 1408, 2, 2048], P('seq', 'tp'), may hold values from -0.125 to 0.125
- fresh_down: float32 [32, 1408, 2048], P('seq', 'tp'), may hold values from -0.15625 to 0.15625
- server_gu: bfloat16 [32, 2816, 2, 2048], P('seq', 'tp'), may hold values from -0.125 to 0.125
- server_down: bfloat16 [32, 2816, 2048], P('seq', 'tp'), may hold values from -0.15625 to 0.15625
Outputs:
- layer_out: bfloat16 [8192, 2048], P('seq', 'tp')
The draws below stay inside these ranges and needn't reach their ends.
Inputs may be any that keep to these rules, and one draw needn't show every extreme that they name: `ctx_len`: some request has exactly 12288 cached positions and some has none. `cache_pos`: -1 marks an empty slot. With a context length L of at most 4096, slot s holds position s for s < L. With a longer context, slots below 4 hold positions 0 to 3 and the other slots hold positions L - 4092 to L - 1, each once. `routes`: each row names 6 different experts; in the rows of one request no expert is named by more than 32 rows, and in every draw some expert by exactly 32. `cache_kv`: keys already carry their position's rotation.
All inputs are finite; a program needn't handle non-finite values.
Results may differ from the reference program's by a relative error of at most 0.025.
Values may be sent and summed in bfloat16 or wider, within the bound.
A program may use at most 128 MiB of HBM per device.

```python
import math
import jax
import jax.numpy as jnp
import numpy as np
from jax import lax

D = 2048
HEADS = 16
HEAD_DIM = 128
EXPERTS = 64
FF = 1408
TOPK = 6
SINK = 4
WIN = 4096
CTXMAX = 12288
NEW = 256
CAP = 32
REQ = 32
HD = 2048
SLOTS = 4096
GROUPS = 4


def context_lengths(key):
    drawn = jax.random.randint(jax.random.fold_in(key, 11), (REQ,), 0, CTXMAX + 1)
    picked = jax.random.permutation(jax.random.fold_in(key, 12), REQ)
    drawn = drawn.at[picked[0]].set(CTXMAX)
    return drawn.at[picked[1]].set(0).astype(jnp.int32)


def draw_ctx_len(key, part):
    return context_lengths(key)


def draw_cache_pos(key, part):
    lengths = context_lengths(key)
    slot_ids = jnp.arange(SLOTS, dtype=jnp.int32)
    cycle_size = SLOTS - SINK
    cycle_base = lengths - cycle_size
    cycle_pos = cycle_base[:, None] + jnp.mod(slot_ids[None, :] - cycle_base[:, None], cycle_size)
    long_pos = jnp.where(slot_ids[None, :] < SINK, slot_ids[None, :], cycle_pos)
    short_pos = jnp.where(slot_ids[None, :] < lengths[:, None], slot_ids[None, :], -1)
    return jnp.where(lengths[:, None] > SLOTS, long_pos, short_pos).astype(jnp.int32)


def draw_cache_kv(key, part):
    drawn_kv = jnp.clip(jax.random.normal(jax.random.fold_in(key, 21), (REQ, SLOTS, 2, HD), jnp.float32), -6.0, 6.0)
    return drawn_kv.astype(jnp.bfloat16)


def place_ends(entries, key, smallest, largest):
    place = [jax.random.randint(jax.random.fold_in(key, axis), (), 0, length) for axis, length in enumerate(entries.shape)]
    main_axis = entries.shape.index(max(entries.shape))
    next_to = place[:main_axis] + [(place[main_axis] + 1) % entries.shape[main_axis]] + place[main_axis + 1:]
    return entries.at[tuple(place)].set(smallest).at[tuple(next_to)].set(largest)


def block_levels(stream_key, extent, shards, smallest, high):
    level = 1.0
    for dim, shards_of in shards:
        steps = jax.random.uniform(jax.random.fold_in(jax.random.fold_in(stream_key, 6), dim), (shards_of,), jnp.float32, smallest / len(shards), high / len(shards))
        level = level * jnp.repeat(jnp.exp(steps), extent[dim] // shards_of).reshape((-1,) + (1,) * (len(extent) - 1 - dim))
    return level


def routed_block(stream_key, own, number, rows, count, top, reach, skew):
    order = jax.random.permutation(stream_key, count)
    heavy_load, common = load_shares(count, rows * top, reach, skew, True), load_shares(count, rows * top, reach, skew, False)
    places = jnp.arange(count)

    def named(sizes, offset_by):
        used = int((sizes > 0).sum())
        fixed = max(1, used // 4)
        shifted = fixed + (places - fixed + offset_by * (used - fixed)) % max(1, count - fixed)
        return jnp.zeros((count,), jnp.int32).at[order[jnp.where(places < fixed, places, shifted)]].set(jnp.asarray(sizes, jnp.int32))

    sizes = jnp.where(number % 4 == 0, named(heavy_load, number // 4), named(common, number - number // 4 - 1))
    mixed = jax.random.permutation(jax.random.fold_in(own, 3), count)
    donor, taker = mixed[0:count // 2 * 2:2], mixed[1:count // 2 * 2:2]
    room = jnp.minimum(sizes[donor] - 1, reach - sizes[taker]) // 2
    room = jnp.where((donor == order[0]) | (taker == order[0]) | (sizes[taker] == 0), 0, jnp.maximum(room, 0))
    shifted = jax.random.randint(jax.random.fold_in(own, 4), (count // 2,), 0, 1 << 20) % (room + 1)
    sizes = sizes.at[donor].add(-shifted).at[taker].add(shifted)
    labels = jnp.searchsorted(jnp.cumsum(sizes), jnp.arange(rows * top), side="right").astype(jnp.int32)
    grid = labels.reshape(top, rows).T
    grid = grid[jax.random.permutation(jax.random.fold_in(own, 1), rows)]
    offset_by = jax.random.randint(jax.random.fold_in(own, 2), (rows, 1), 0, top)
    return jnp.take_along_axis(grid, (jnp.arange(top)[None, :] + offset_by) % top, axis=1)


def load_shares(amount, total, bound, slope, full):
    portions = [(1 << 20) // math.isqrt(rank ** slope) + 1 for rank in range(1, amount + 1)]
    largest = bound if full else min(bound, max(-(-total // amount), total * portions[0] // sum(portions)))
    least = 1 if total - largest >= amount - 1 else 0
    counts, spare = [largest] + [least] * (amount - 1), total - largest - least * (amount - 1)
    while spare > 0:
        movable = [i for i in range(1, amount) if counts[i] < largest] or [i for i in range(1, amount) if counts[i] < bound]
        whole, left = sum([portions[i] for i in movable]), spare
        for i in movable:
            extra = min(bound - counts[i], max(1, left * portions[i] // whole), spare)
            counts[i] = counts[i] + extra
            spare = spare - extra
    return np.array(counts)


def scatter_about(rng, dims, spread, bound, pieces=(), held_as=jnp.bfloat16):
    gain = block_levels(rng, dims, pieces, -0.22, 0.18) if pieces else 1.0
    array = jax.random.normal(rng, dims, jnp.float32) * spread * gain
    return jnp.minimum(jnp.maximum(array, -bound), bound).astype(held_as)


def setup_inputs(seed: int = 0) -> dict:
    key_list = jax.random.split(jax.random.key(seed), 16)
    tokens = scatter_about(key_list[0], (REQ * NEW, D), 1.0, 6.0, ((0, 32), (1, 8)))
    ctx_len = draw_ctx_len(jax.random.fold_in(key_list[15], 71), 0)
    cache_kv = draw_cache_kv(jax.random.fold_in(key_list[15], 71), 0)
    cache_pos = draw_cache_pos(jax.random.fold_in(key_list[15], 71), 0)
    attn_gain = jnp.clip(1.0 + 0.1 * jax.random.normal(key_list[4], (D,), jnp.float32), 0.5, 1.5)
    moe_gain = jnp.clip(1.0 + 0.1 * jax.random.normal(key_list[5], (D,), jnp.float32), 0.5, 1.5)
    qkv_train = scatter_about(key_list[6], (D, 3, HD), D ** -0.5, 0.125, ((0, 32), (2, 8)), jnp.float32)
    out_train = scatter_about(key_list[7], (D, HD), HD ** -0.5, 0.125, ((0, 32), (1, 8)), jnp.float32)
    router = scatter_about(key_list[8], (D, EXPERTS), D ** -0.5, 0.125)
    routes_keys = jax.random.split(jax.random.fold_in(key_list[9], 1), (REQ * NEW) // NEW)
    routes_turns = jax.random.permutation(jax.random.fold_in(key_list[9], 3), (REQ * NEW) // NEW)
    routes = jax.vmap(lambda own, number: routed_block(jax.random.fold_in(key_list[9], 2), own, number, NEW, EXPERTS, TOPK, CAP, 2))(routes_keys, routes_turns).reshape((REQ * NEW, TOPK))
    handed_half = place_ends(jax.random.randint(key_list[10], (EXPERTS // 2,), 0, 2), jax.random.fold_in(key_list[10], 1), 0, 1).astype(jnp.int32)
    fresh_gu = scatter_about(key_list[11], (EXPERTS // 2, FF, 2, D), D ** -0.5, 0.125, ((0, 32), (1, 8)), jnp.float32)
    fresh_down = scatter_about(key_list[12], (EXPERTS // 2, FF, D), FF ** -0.5, 0.15625, ((0, 32), (1, 8)), jnp.float32)
    server_gu = scatter_about(key_list[13], (EXPERTS // 2, 2 * FF, 2, D), D ** -0.5, 0.125, ((0, 32), (1, 8)))
    server_down = scatter_about(key_list[14], (EXPERTS // 2, 2 * FF, D), FF ** -0.5, 0.15625, ((0, 32), (1, 8)))
    return dict(tokens=tokens, ctx_len=ctx_len, cache_kv=cache_kv, cache_pos=cache_pos, attn_gain=attn_gain, moe_gain=moe_gain, qkv_train=qkv_train, out_train=out_train, router=router, routes=routes, handed_half=handed_half, fresh_gu=fresh_gu, fresh_down=fresh_down, server_gu=server_gu, server_down=server_down)


def normed(field, gain_vec):
    values_in = field.astype(jnp.float32)
    inv_rms = lax.rsqrt(lax.optimization_barrier(jnp.mean(values_in * values_in, axis=-1, keepdims=True)) + 1e-06)
    return (values_in * inv_rms * gain_vec).astype(jnp.bfloat16)

def rotate(field, positions):
    half_dim = field.shape[-1] // 2
    frequency = 10000.0 ** (-jnp.arange(half_dim, dtype=jnp.float32) / half_dim)
    angles = positions.astype(jnp.float32)[:, None] * frequency[None, :]
    cosine = jnp.cos(angles)[:, None, :]
    sine = jnp.sin(angles)[:, None, :]
    first_half = field[..., :half_dim]
    second_half = field[..., half_dim:]
    return jnp.concatenate([first_half * cosine - second_half * sine, second_half * cosine + first_half * sine], axis=-1)

def attend(queries, keys_new, values_new, cache_keys, cache_values, slot_pos, context):
    new_count = queries.shape[0]
    key_all = jnp.concatenate([cache_keys, keys_new], axis=0).astype(jnp.float32)
    value_all = jnp.concatenate([cache_values, values_new], axis=0).astype(jnp.float32)
    scores = jnp.einsum('qhd,khd->hqk', queries.astype(jnp.float32), key_all) / jnp.sqrt(jnp.float32(HEAD_DIM))
    token_ids = jnp.arange(new_count, dtype=jnp.int32)
    positions = context + token_ids
    cache_ok = (slot_pos[None, :] >= 0) & ((slot_pos[None, :] < SINK) | (positions[:, None] - slot_pos[None, :] < WIN))
    new_ok = token_ids[None, :] <= token_ids[:, None]
    allowed = jnp.concatenate([cache_ok, new_ok], axis=1)
    scores = jnp.where(allowed[None], scores, jnp.float32(-1e+30))
    row_top = lax.optimization_barrier(jnp.max(scores, axis=-1, keepdims=True))
    weights = jnp.exp(scores - row_top)
    row_total = lax.optimization_barrier(jnp.sum(weights, axis=-1, keepdims=True))
    probability = (weights / row_total).astype(jnp.bfloat16)
    return jnp.einsum('hqk,khd->qhd', probability.astype(jnp.float32), value_all).astype(jnp.bfloat16)

def reference(tokens, ctx_len, cache_kv, cache_pos, attn_gain, moe_gain, qkv_train, out_train, router, routes, handed_half, fresh_gu, fresh_down, server_gu, server_down):
    qkv_weight = qkv_train.astype(jnp.bfloat16)
    out_weight = out_train.astype(jnp.bfloat16)
    normed_x = normed(tokens, attn_gain)
    projected = jnp.dot(normed_x, qkv_weight.reshape(D, 3 * HD), preferred_element_type=jnp.float32)
    projected = projected.reshape(REQ, NEW, 3, HEADS, HEAD_DIM)

    def one_request(packed):
        proj_req, context, cache_req, slot_pos = packed
        positions = context + jnp.arange(NEW, dtype=jnp.int32)
        queries = rotate(proj_req[:, 0], positions).astype(jnp.bfloat16)
        keys_new = rotate(proj_req[:, 1], positions).astype(jnp.bfloat16)
        values_new = proj_req[:, 2].astype(jnp.bfloat16)
        cached = cache_req.reshape(SLOTS, 2, HEADS, HEAD_DIM)
        mixed = attend(queries, keys_new, values_new, cached[:, 0], cached[:, 1], slot_pos, context)
        return mixed.reshape(NEW, HD)
    mixed_heads = lax.map(one_request, (projected, ctx_len, cache_kv, cache_pos)).reshape(REQ * NEW, HD)
    attn_total = lax.dot_general(mixed_heads, out_weight, (((1,), (1,)), ((), ())), preferred_element_type=jnp.float32)
    hidden_state = (tokens.astype(jnp.float32) + attn_total).astype(jnp.bfloat16)
    moe_in = normed(hidden_state, moe_gain)
    logits = jnp.dot(moe_in, router, preferred_element_type=jnp.float32)
    gate_values = jax.nn.sigmoid(jnp.take_along_axis(logits, routes, axis=1))
    tok_total = REQ * NEW
    max_rows = REQ * CAP
    group_units = FF // GROUPS
    fresh_gu_b = fresh_gu.astype(jnp.bfloat16)
    fresh_down_b = fresh_down.astype(jnp.bfloat16)
    server_gu_v = server_gu.reshape(EXPERTS // 2, GROUPS, 2, group_units, 2, D)
    server_down_v = server_down.reshape(EXPERTS // 2, GROUPS, 2, group_units, D)
    token_ids = jnp.arange(tok_total, dtype=jnp.int32)

    def one_expert(combined, expert_id):
        parity = expert_id % 2
        pair_index = expert_id // 2
        use_fresh = parity == handed_half[pair_index]
        server_pick = lax.dynamic_index_in_dim(server_gu_v[pair_index], parity, 1, keepdims=False).reshape(FF, 2, D)
        down_pick = lax.dynamic_index_in_dim(server_down_v[pair_index], parity, 1, keepdims=False).reshape(FF, D)
        w_gu = jnp.where(use_fresh, fresh_gu_b[pair_index], server_pick)
        w_down = jnp.where(use_fresh, fresh_down_b[pair_index], down_pick)
        route_hit = routes == expert_id
        routed = jnp.any(route_hit, axis=1)
        gate_expert = lax.optimization_barrier(jnp.sum(jnp.where(route_hit, gate_values, jnp.float32(0.0)), axis=1))
        sort_key = jnp.where(routed, token_ids, token_ids + tok_total)
        row_order = jnp.argsort(sort_key)[:max_rows].astype(jnp.int32)
        rows_in = moe_in[row_order]
        gate_pre = lax.dot_general(rows_in, w_gu[:, 0], (((1,), (1,)), ((), ())), preferred_element_type=jnp.float32)
        up_pre = lax.dot_general(rows_in, w_gu[:, 1], (((1,), (1,)), ((), ())), preferred_element_type=jnp.float32)
        activated = (jax.nn.silu(gate_pre) * up_pre).astype(jnp.bfloat16)
        grouped = activated.astype(jnp.float32).reshape(max_rows, GROUPS, group_units)
        down_grouped = w_down.astype(jnp.float32).reshape(GROUPS, group_units, D)
        partial_out = jnp.einsum('mgf,gfd->gmd', grouped, down_grouped)
        rounded = lax.optimization_barrier(partial_out.astype(jnp.bfloat16)).astype(jnp.float32)
        expert_out = lax.optimization_barrier(jnp.sum(rounded, axis=0)).astype(jnp.bfloat16)
        weight_rows = jnp.where(routed, gate_expert, jnp.float32(0.0))[row_order]
        combined = combined.at[row_order].add(weight_rows[:, None] * expert_out.astype(jnp.float32))
        return (combined, None)
    combined, _ = lax.scan(one_expert, jnp.zeros((tok_total, D), jnp.float32), jnp.arange(EXPERTS, dtype=jnp.int32))
    return (hidden_state.astype(jnp.float32) + combined).astype(jnp.bfloat16)
```

```python
import functools

import jax
import jax.numpy as jnp
from jax import lax
from jax.experimental import pallas as pl
from jax.experimental.pallas import tpu as pltpu
from jax.sharding import PartitionSpec as P

HEAD_DIM = 128
SINK = 4
WIN = 4096
MESH = pl.DeviceIdType.MESH
BF = jnp.bfloat16
F32 = jnp.float32
ANY = pl.BlockSpec(memory_space=pl.ANY)
VMEM = pl.BlockSpec(memory_space=pltpu.VMEM)
SMEM = pl.BlockSpec(memory_space=pltpu.SMEM)
DMA = pltpu.SemaphoreType.DMA
ORDER = (0, 1, 7, 2, 6, 3, 5, 4)


def places():
    return lax.axis_index("seq"), lax.axis_index("tp")


def greet(peers):
    barrier = pltpu.get_barrier_semaphore()
    for peer in peers:
        pl.semaphore_signal(barrier, inc=1, device_id=peer, device_id_type=MESH)
    pl.semaphore_wait(barrier, len(peers))


def push(src, dst, send, recv, peer):
    copy = pltpu.make_async_remote_copy(
        src_ref=src, dst_ref=dst, send_sem=send, recv_sem=recv, device_id=peer, device_id_type=MESH
    )
    copy.start()
    return copy


def tp_peers(s, t):
    return [(s, t ^ k) for k in range(1, 8)]


def seq_peer(s, t, k, j):
    z, r = s // 4, s % 4
    return ((z + k) % 8) * 4 + (r ^ j), t


def gather_kernel(tok, w, tok_all, w_all, lsem, tok_s, tok_r, x_s, x_r, z_s, z_r, c_s, c_r):
    s, t = places()
    z, xh, c = s // 4, (s // 2) % 2, s % 2
    up = (((z + 1) % 8) * 4 + xh * 2 + c, t)
    down = (((z + 7) % 8) * 4 + xh * 2 + c, t)
    over = (s ^ 2, t)
    twin = (s ^ 1, t)
    greet(tp_peers(s, t) + [up, down, over, twin])

    def block(dz, a):
        return w_all.at[(z + dz) % 8, xh ^ a, c]

    own = w.at[:, :]
    home = w_all.at[z, xh, c]
    waits = [push(own, home, x_s, x_r, over)]
    ups = {(0, 0): push(own, home, z_s.at[0, 0, 0], z_r.at[0, 0, 0], up)}
    downs = {(0, 0): push(own, home, z_s.at[1, 0, 0], z_r.at[1, 0, 0], down)}
    twins = [push(own, home, c_s.at[0, 0], c_r.at[0, 0], twin)]
    local_w = pltpu.make_async_copy(own, home, lsem.at[0])
    local_w.start()
    mine = tok_all.at[:, pl.ds(pl.multiple_of(t * 256, 256), 256)]
    local_t = pltpu.make_async_copy(tok, mine, lsem.at[1])
    local_t.start()
    toks = [push(tok, mine, tok_s.at[k], tok_r.at[k], (s, t ^ k)) for k in range(1, 8)]

    waits[0].wait_recv()
    theirs = block(0, 1)
    ups[(0, 1)] = push(theirs, theirs, z_s.at[0, 0, 1], z_r.at[0, 0, 1], up)
    downs[(0, 1)] = push(theirs, theirs, z_s.at[1, 0, 1], z_r.at[1, 0, 1], down)
    twins.append(push(theirs, theirs, c_s.at[0, 1], c_r.at[0, 1], twin))

    for step in range(4):
        for a in range(2):
            for way, (chain, peer, dz) in enumerate(((ups, up, -1 - step), (downs, down, 1 + step))):
                if (step, a) not in chain:
                    continue
                chain[(step, a)].wait_recv()
                here = block(dz + 8, a)
                if step < 2 or (step == 2 and a == way):
                    chain[(step + 1, a)] = push(
                        here, here, z_s.at[way, step + 1, a], z_r.at[way, step + 1, a], peer
                    )
                place = (dz + 8) % 8
                twins.append(push(here, here, c_s.at[place, a], c_r.at[place, a], twin))
    for copy in twins + toks:
        copy.wait()
    for copy in list(ups.values()) + list(downs.values()) + waits:
        copy.wait_send()
    local_w.wait()
    local_t.wait()


def gather(tok, w):
    return pl.pallas_call(
        gather_kernel,
        out_shape=(
            jax.ShapeDtypeStruct((256, 2048), BF),
            jax.ShapeDtypeStruct((8, 2, 2, 64, 1024), BF),
        ),
        in_specs=[ANY, ANY],
        out_specs=(ANY, ANY),
        scratch_shapes=[
            DMA((2,)),
            DMA((8,)),
            DMA((8,)),
            DMA,
            DMA,
            DMA((2, 4, 2)),
            DMA((2, 4, 2)),
            DMA((8, 2)),
            DMA((8, 2)),
        ],
        compiler_params=pltpu.CompilerParams(collective_id=0, has_side_effects=True),
        name="gather_inputs",
    )(tok, w)


def split_matrix(n):
    row = lax.broadcasted_iota(jnp.int32, (n, n), 0)
    col = lax.broadcasted_iota(jnp.int32, (n, n), 1)
    half = n // 2
    return jnp.where(col == jnp.where(row < half, 2 * row, 2 * (row - half) + 1), 1.0, 0.0).astype(BF)


def nt(a, b):
    return lax.dot_general(a, b, (((1,), (1,)), ((), ())), preferred_element_type=F32)


def attention_kernel(
    tok, w, gain, cosf, sinf, limit, cache, out, buf, vals, scores, top, total, acc, xn, sem
):
    chunks, width = 8, 512

    def fetch(i, h):
        rows = pl.ds(pl.multiple_of(i * width, width), width)
        return pltpu.make_async_copy(
            cache.at[rows, :, pl.ds(h * 128, 128)], buf.at[h, rows], sem.at[i, h]
        )

    for i in range(chunks):
        for h in range(2):
            fetch(i, h).start()
    field = tok[...].astype(F32)
    inv = lax.rsqrt(jnp.mean(field * field, axis=-1, keepdims=True) + 1e-6)
    xn[...] = (field * inv * gain[...]).astype(BF)
    projected = jnp.dot(xn[...], w[:, 0:768], preferred_element_type=F32)

    def turned(part):
        return (part * cosf[...] + pltpu.roll(part, 64, 1) * sinf[...]).astype(BF)

    queries = [turned(projected[:, h * 128 : h * 128 + 128]) for h in range(2)]
    keys_new = [turned(projected[:, 256 + h * 128 : 384 + h * 128]) for h in range(2)]
    values_new = [projected[:, 512 + h * 128 : 640 + h * 128].astype(BF) for h in range(2)]
    perm = split_matrix(256)
    row_id = lax.broadcasted_iota(jnp.int32, (256, width), 0)
    flat = [buf.at[h].reshape(8192, 128) for h in range(2)]

    new_row = lax.broadcasted_iota(jnp.int32, (256, 256), 0)
    new_col = lax.broadcasted_iota(jnp.int32, (256, 256), 1)
    for h in range(2):
        fresh = jnp.where(new_col <= new_row, nt(queries[h], keys_new[h]), -1e30)
        scores[h, chunks, :, 0:256] = fresh
        top[h] = jnp.maximum(fresh[:, 0:128], fresh[:, 128:256])

    @pl.loop(0, chunks)
    def _(i):
        for h in range(2):
            fetch(i, h).wait()
        keys = [[], []]
        for part in range(4):
            start = pl.multiple_of(i * 1024 + part * 256, 256)
            both = jnp.concatenate([flat[h][pl.ds(start, 256), :] for h in range(2)], axis=1)
            split = jnp.dot(perm, both, preferred_element_type=F32).astype(BF)
            spot = pl.multiple_of(i * width + part * 128, 128)
            vals[pl.ds(spot, 128), :] = split[128:256]
            for h in range(2):
                keys[h].append(split[0:128, h * 128 : h * 128 + 128])
        seen = row_id < limit[:, pl.ds(pl.multiple_of(i * width, width), width)]
        for h in range(2):
            key_block = jnp.concatenate(keys[h], axis=0)
            block = jnp.where(seen, nt(queries[h], key_block), -1e30)
            scores[h, i] = block
            peak = jnp.maximum(
                jnp.maximum(block[:, 0:128], block[:, 128:256]),
                jnp.maximum(block[:, 256:384], block[:, 384:512]),
            )
            top[h] = jnp.maximum(top[h], peak)

    scale = 1.4426950408889634 / (HEAD_DIM**0.5)
    for h in range(2):
        top[h] = jnp.broadcast_to(jnp.max(top[h], axis=1, keepdims=True), (256, 128))
        peak = top[h]
        weights = jnp.exp2((scores[h, chunks, :, 0:256] - jnp.tile(peak, (1, 2))) * scale)
        total[h] = weights[:, 0:128] + weights[:, 128:256]
        acc[h] = jnp.dot(weights.astype(BF), values_new[h], preferred_element_type=F32)

    @pl.loop(0, chunks)
    def _(i):
        for h in range(2):
            weights = jnp.exp2((scores[h, i] - jnp.tile(top[h], (1, 4))) * scale)
            total[h] += (weights[:, 0:128] + weights[:, 128:256]) + (
                weights[:, 256:384] + weights[:, 384:512]
            )
            spots = pl.ds(pl.multiple_of(i * width, width), width)
            acc[h] += jnp.dot(
                weights.astype(BF), vals[spots, h * 128 : h * 128 + 128], preferred_element_type=F32
            )

    mixed = jnp.concatenate(
        [(acc[h] / jnp.sum(total[h], axis=1, keepdims=True)).astype(BF) for h in range(2)], axis=1
    )
    for part in range(8):
        out[part] = nt(mixed, w[part * 256 : part * 256 + 256, 768:1024]).astype(BF)


def attention(tok, w, gain, cosf, sinf, limit, cache):
    return pl.pallas_call(
        attention_kernel,
        out_shape=jax.ShapeDtypeStruct((8, 256, 256), BF),
        in_specs=[VMEM] * 6 + [ANY],
        out_specs=VMEM,
        scratch_shapes=[
            pltpu.VMEM((2, 4096, 2, 128), BF),
            pltpu.VMEM((4096, 256), BF),
            pltpu.VMEM((2, 9, 256, 512), F32),
            pltpu.VMEM((2, 256, 128), F32),
            pltpu.VMEM((2, 256, 128), F32),
            pltpu.VMEM((2, 256, 128), F32),
            pltpu.VMEM((256, 2048), BF),
            DMA((8, 2)),
        ],
        compiler_params=pltpu.CompilerParams(vmem_limit_bytes=48 << 20),
        name="attention",
    )(tok, w, gain, cosf, sinf, limit, cache)


def scatter_sum_kernel(part, got, lsem, ssem, rsem):
    s, t = places()
    greet(tp_peers(s, t))
    local = pltpu.make_async_copy(part.at[t], got.at[t], lsem)
    local.start()
    copies = [push(part.at[t ^ k], got.at[t], ssem.at[k], rsem.at[k], (s, t ^ k)) for k in range(1, 8)]
    for copy in copies:
        copy.wait()
    local.wait()


def scatter_sum(part):
    return pl.pallas_call(
        scatter_sum_kernel,
        out_shape=jax.ShapeDtypeStruct((8, 256, 256), BF),
        in_specs=[ANY],
        out_specs=ANY,
        scratch_shapes=[DMA, DMA((8,)), DMA((8,))],
        compiler_params=pltpu.CompilerParams(collective_id=1, has_side_effects=True),
        name="project_exchange",
    )(part)


def slot_rows(rank, first):
    shelf = lax.broadcasted_iota(jnp.int32, (32, 256), 0).astype(F32)
    return [jnp.where(rank[first + e : first + e + 1, :] == shelf, 1.0, 0.0) for e in range(8)]


def send_rows_kernel(got, tok, rank, routes, router, gain, hidden, rows, stats):
    total = tok[...].astype(F32)
    part = got[0].astype(F32)
    for k in range(1, 8):
        part += got[k].astype(F32)
    state = (total + part).astype(BF)
    hidden[...] = state
    for chunk in range(8):
        pick = jnp.concatenate(slot_rows(rank, chunk * 8), axis=0).astype(BF)
        rows[chunk] = jnp.dot(pick, state, preferred_element_type=F32).astype(BF)
    wide = state.astype(F32)
    logits = nt(router[...], (wide * gain[...]).astype(BF))
    expert = lax.broadcasted_iota(jnp.int32, (64, 256), 0)
    lines = [
        jnp.sum(jnp.where(routes[k : k + 1, :] == expert, logits, 0.0), axis=0, keepdims=True)
        for k in range(6)
    ]
    square = jnp.sum(jnp.transpose(wide * wide), axis=0, keepdims=True)
    stats[...] = jnp.concatenate(lines + [square, jnp.zeros((1, 256), F32)], axis=0)


def send_rows(got, tok, rank, routes, router, gain):
    return pl.pallas_call(
        send_rows_kernel,
        out_shape=(
            jax.ShapeDtypeStruct((256, 256), BF),
            jax.ShapeDtypeStruct((8, 256, 256), BF),
            jax.ShapeDtypeStruct((8, 256), F32),
        ),
        in_specs=[VMEM] * 6,
        out_specs=(VMEM,) * 3,
        name="send_rows",
    )(got, tok, rank, routes, router, gain)


def dispatch_kernel(rows, stats, x, stats_all, stage, lsem, a_s, a_r, b_s, b_r, g_s, g_r):
    s, t = places()
    z, r = s // 4, s % 4
    far = [seq_peer(s, t, k, j) for k in range(8) for j in range(4) if (k, j) != (0, 0)]
    greet(tp_peers(s, t) + far)
    sends = []
    own = pltpu.make_async_copy(rows.at[:, s], stage.at[:, s], lsem.at[0])
    own.start()
    for k in ORDER:
        for j in range(4):
            if (k, j) == (0, 0):
                continue
            peer = seq_peer(s, t, k, j)
            sends.append(push(rows.at[:, peer[0]], stage.at[:, s], a_s.at[k, j], a_r.at[k, j], peer))
    small = [push(stats, stats_all.at[t], g_s.at[k], g_r.at[k], (s, t ^ k)) for k in range(1, 8)]
    near = pltpu.make_async_copy(stats, stats_all.at[t], lsem.at[1])
    near.start()
    columns = pl.ds(pl.multiple_of(t * 256, 256), 256)
    forwards = []
    locals_ = []
    for k in ORDER:
        group = (z + 8 - k) % 8
        here = pl.ds(group * 4, 4)
        for j in range(4):
            if (k, j) == (0, 0):
                own.wait()
            else:
                source = group * 4 + (r ^ j)
                pltpu.make_async_copy(stage.at[:, source], stage.at[:, source], a_r.at[k, j]).wait()
        target = x.at[here, :, columns]
        for m in range(1, 8):
            forwards.append(
                push(stage.at[(t ^ m) % 2, here], target, b_s.at[k, m], b_r.at[k, m], (s, t ^ m))
            )
        keep = pltpu.make_async_copy(stage.at[t % 2, here], target, b_s.at[k, 0])
        keep.start()
        locals_.append(keep)
    for copy in sends:
        copy.wait_send()
    for copy in forwards + small:
        copy.wait()
    for copy in locals_:
        copy.wait()
    near.wait()


def dispatch(rows, stats):
    return pl.pallas_call(
        dispatch_kernel,
        out_shape=(
            jax.ShapeDtypeStruct((32, 32, 2048), BF),
            jax.ShapeDtypeStruct((8, 8, 256), F32),
        ),
        in_specs=[ANY, ANY],
        out_specs=(ANY, ANY),
        scratch_shapes=[
            pltpu.VMEM((2, 32, 32, 256), BF),
            DMA((2,)),
            DMA((8, 4)),
            DMA((8, 4)),
            DMA((8, 8)),
            DMA((8, 8)),
            DMA((8,)),
            DMA((8,)),
        ],
        compiler_params=pltpu.CompilerParams(collective_id=2, has_side_effects=True),
        name="dispatch",
    )(rows, stats)


def experts_kernel(
    flags, x, gain, s_gu, s_down, a_gu, a_down, b_gu, b_down, y, wbuf, wdown, weights, xn, sem
):
    def fetch(gu, down, first, count, slot):
        copies = []
        for col in range(16):
            copies.append(
                pltpu.make_async_copy(
                    gu.at[:, :, pl.ds(col * 128, 128)],
                    wbuf.at[col, pl.ds(first, count)],
                    sem.at[slot, col],
                )
            )
        copies.append(
            pltpu.make_async_copy(down, wdown.at[pl.ds(first, count)], sem.at[slot, 16])
        )
        return copies

    fresh = flags[0] == 1
    low = pl.multiple_of(flags[1] * 176, 16)
    high = pl.multiple_of(176 - flags[1] * 176, 16)

    def both():
        return fetch(a_gu, a_down, low, 176, 0) + fetch(b_gu, b_down, high, 176, 1)

    def single():
        return fetch(s_gu, s_down, 0, 352, 0)

    @pl.when(fresh)
    def _():
        for copy in both():
            copy.start()

    @pl.when(jnp.logical_not(fresh))
    def _():
        for copy in single():
            copy.start()

    @pl.loop(0, 16)
    def _(i):
        span = pl.ds(pl.multiple_of(i * 64, 64), 64)
        field = x[span, :].astype(F32)
        inv = lax.rsqrt(jnp.mean(field * field, axis=-1, keepdims=True) + 1e-6)
        xn[span, :] = (field * inv * gain[...]).astype(BF)

    @pl.when(fresh)
    def _():
        for copy in both():
            copy.wait()

    @pl.when(jnp.logical_not(fresh))
    def _():
        for copy in single():
            copy.wait()

    flat = wbuf.reshape(16, 704, 128)
    for first, count in ((0, 256), (256, 256), (512, 192)):
        perm = split_matrix(count)
        half = count // 2
        for col in range(8):
            pair = jnp.concatenate(
                [flat[2 * col + i, first : first + count, :] for i in range(2)], axis=1
            )
            split = jnp.dot(perm, pair, preferred_element_type=F32).astype(BF)
            for kind in range(2):
                weights[kind, first // 2 : first // 2 + half, col * 256 : col * 256 + 256] = split[
                    kind * half : kind * half + half
                ]

    @pl.loop(0, 8)
    def _(i):
        span = pl.ds(pl.multiple_of(i * 128, 128), 128)
        block = xn[span, :]
        gate = nt(block, weights[0])
        up = nt(block, weights[1])
        act = (gate / (1.0 + jnp.exp(-gate)) * up).astype(BF)
        result = jnp.dot(act, wdown[...], preferred_element_type=F32).astype(BF)
        for part in range(8):
            y[part, span, :] = result[:, part * 256 : part * 256 + 256]


def experts(flags, x, gain, *weights):
    return pl.pallas_call(
        experts_kernel,
        out_shape=jax.ShapeDtypeStruct((8, 1024, 256), BF),
        in_specs=[SMEM, VMEM, VMEM] + [ANY] * 6,
        out_specs=VMEM,
        scratch_shapes=[
            pltpu.VMEM((16, 352, 2, 128), BF),
            pltpu.VMEM((352, 2048), BF),
            pltpu.VMEM((2, 352, 2048), BF),
            pltpu.VMEM((1024, 2048), BF),
            DMA((2, 17)),
        ],
        compiler_params=pltpu.CompilerParams(vmem_limit_bytes=48 << 20),
        name="experts",
    )(flags, x, gain, *weights)


def return_kernel(y, back, tbuf, sums, lsem, a_s, a_r, b_s, b_r):
    s, t = places()
    z, r = s // 4, s % 4
    far = [seq_peer(s, t, k, j) for k in range(8) for j in range(4) if (k, j) != (0, 0)]
    greet(tp_peers(s, t) + far)
    firsts, locals_ = [], []
    for k in ORDER:
        here = pl.ds(((z + k) % 8) * 4, 4)
        for m in range(1, 8):
            firsts.append(
                push(y.at[t ^ m, here], tbuf.at[t, here], a_s.at[k, m], a_r.at[k, m], (s, t ^ m))
            )
        keep = pltpu.make_async_copy(y.at[t, here], tbuf.at[t, here], lsem.at[k])
        keep.start()
        locals_.append(keep)
    seconds = []
    last = None
    for place, k in enumerate(ORDER):
        group = ((z + k) % 8) * 4
        here = pl.ds(group, 4)
        for copy in firsts[place * 7 : place * 7 + 7]:
            copy.wait_recv()
        locals_[place].wait()
        for par in range(2):
            first = tbuf[par, here].astype(F32) + tbuf[par + 2, here].astype(F32)
            second = tbuf[par + 4, here].astype(F32) + tbuf[par + 6, here].astype(F32)
            sums[par, here] = (first + second).astype(BF)
        for j in range(4):
            target = group + (r ^ j)
            if (k, j) == (0, 0):
                last = pltpu.make_async_copy(sums.at[:, target], back.at[:, s], lsem.at[8])
                last.start()
            else:
                seconds.append(
                    push(sums.at[:, target], back.at[:, s], b_s.at[k, j], b_r.at[k, j], (target, t))
                )
    for copy in firsts:
        copy.wait_send()
    for copy in seconds:
        copy.wait()
    last.wait()


def give_back(y):
    return pl.pallas_call(
        return_kernel,
        out_shape=jax.ShapeDtypeStruct((2, 32, 32, 256), BF),
        in_specs=[ANY],
        out_specs=ANY,
        scratch_shapes=[
            pltpu.VMEM((8, 32, 32, 256), BF),
            pltpu.VMEM((2, 32, 32, 256), BF),
            DMA((9,)),
            DMA((8, 8)),
            DMA((8, 8)),
            DMA((8, 4)),
            DMA((8, 4)),
        ],
        compiler_params=pltpu.CompilerParams(
            collective_id=3, has_side_effects=True, vmem_limit_bytes=24 << 20
        ),
        name="give_back",
    )(y)


def combine_kernel(back, hidden, rank, routes, stats, out):
    lines = stats[0]
    for k in range(1, 8):
        lines += stats[k]
    inv = lax.rsqrt(lines[6:7, :] * (1.0 / 2048.0) + 1e-6)
    gate = 1.0 / (1.0 + jnp.exp(-(lines * inv)))
    shelf = lax.broadcasted_iota(jnp.int32, (64, 256), 0)
    expert = (shelf % 32) * 2 + shelf // 32
    share = jnp.zeros((64, 256), F32)
    for k in range(6):
        share += jnp.where(routes[k : k + 1, :] == expert, gate[k : k + 1, :], 0.0)
    total = hidden[...].astype(F32)
    for chunk in range(8):
        pick = slot_rows(rank, chunk * 8)
        mix = jnp.concatenate(
            [pick[e] * share[chunk * 8 + e : chunk * 8 + e + 1, :] for e in range(8)], axis=0
        )
        high = mix.astype(BF)
        low = (mix - high.astype(F32)).astype(BF)
        dims = (((0,), (0,)), ((), ()))
        total += lax.dot_general(high, back[chunk], dims, preferred_element_type=F32)
        total += lax.dot_general(low, back[chunk], dims, preferred_element_type=F32)
    out[...] = total.astype(BF)


def combine(back, hidden, rank, routes, stats):
    return pl.pallas_call(
        combine_kernel,
        out_shape=jax.ShapeDtypeStruct((256, 256), BF),
        in_specs=[VMEM] * 5,
        out_specs=VMEM,
        name="combine",
    )(back, hidden, rank, routes, stats)


def swapped(array):
    return lax.ppermute(array, "tp", [(i, i ^ 1) for i in range(8)])


def body(
    tokens,
    ctx_len,
    cache_kv,
    cache_pos,
    attn_gain,
    moe_gain,
    qkv_train,
    out_train,
    router,
    routes,
    handed_half,
    fresh_gu,
    fresh_down,
    server_gu,
    server_down,
):
    t = lax.axis_index("tp")
    s = lax.axis_index("seq")
    own_gu = fresh_gu[0].astype(BF)
    own_down = fresh_down[0].astype(BF)
    other_gu, other_down = swapped((own_gu, own_down))
    shard = jnp.concatenate([qkv_train.reshape(64, 768), out_train], axis=1).astype(BF)
    tok_all, w_all = gather(tokens, shard)

    context = ctx_len[0]
    half = HEAD_DIM // 2
    frequency = 10000.0 ** (-jnp.arange(half, dtype=F32) / half)
    positions = context + jnp.arange(256, dtype=jnp.int32)
    angles = positions.astype(F32)[:, None] * frequency[None, :]
    cosine, sine = jnp.cos(angles), jnp.sin(angles)
    cosf = jnp.concatenate([cosine, cosine], axis=1)
    sinf = jnp.concatenate([-sine, sine], axis=1)
    slot = cache_pos
    limit = jnp.where(slot < 0, 0, jnp.where(slot < SINK, 256, slot + WIN - context))
    part = attention(
        tok_all,
        w_all.reshape(2048, 1024),
        attn_gain.reshape(1, 2048),
        cosf,
        sinf,
        limit,
        cache_kv[0],
    )
    got = scatter_sum(part)

    routes_t = routes.T
    shelf = jnp.arange(64, dtype=jnp.int32)
    named = (shelf % 32) * 2 + shelf // 32
    hit = jnp.any(routes_t[None, :, :] == named[:, None, None], axis=1)
    later = (jnp.arange(256)[:, None] < jnp.arange(256)[None, :]).astype(BF)
    before = jnp.dot(hit.astype(BF), later, preferred_element_type=F32)
    rank = jnp.where(hit, before, -1.0)

    columns = t * 256
    gain_part = lax.dynamic_slice_in_dim(moe_gain, columns, 256, 0).reshape(1, 256)
    router_part = lax.dynamic_slice_in_dim(router, columns, 256, 0).T
    hidden, rows, stats = send_rows(got, tokens, rank, routes_t, router_part, gain_part)
    x, stats_all = dispatch(rows.reshape(2, 32, 32, 256), stats)

    parity = t % 2
    use_fresh = lax.dynamic_index_in_dim(handed_half, s, 0, keepdims=False) == parity
    flags = jnp.stack([use_fresh.astype(jnp.int32), parity.astype(jnp.int32)])
    y = experts(
        flags,
        x.reshape(1024, 2048),
        moe_gain.reshape(1, 2048),
        server_gu[0],
        server_down[0],
        own_gu,
        own_down,
        other_gu,
        other_down,
    )
    back = give_back(y.reshape(8, 32, 32, 256))
    return combine(back.reshape(8, 256, 256), hidden, rank, routes_t, stats_all)


def solution(mesh):
    placed = (
        P("seq", "tp"),
        P("seq"),
        P("seq", None, None, "tp"),
        P("seq", None),
        P(),
        P(),
        P("seq", None, "tp"),
        P("seq", "tp"),
        P(),
        P("seq", None),
        P(),
        P("seq", "tp", None, None),
        P("seq", "tp", None),
        P("seq", "tp", None, None),
        P("seq", "tp", None),
    )
    return jax.shard_map(
        body, mesh=mesh, in_specs=placed, out_specs=P("seq", "tp"), check_vma=False
    )
```

```python
import functools

import jax
import jax.numpy as jnp
from jax import lax
from jax.experimental import pallas as pl
from jax.experimental.pallas import tpu as pltpu
from jax.sharding import PartitionSpec as P

HEAD_DIM = 128
SINK = 4
WIN = 4096
MESH = pl.DeviceIdType.MESH
BF = jnp.bfloat16
F32 = jnp.float32
ANY = pl.BlockSpec(memory_space=pl.ANY)
VMEM = pl.BlockSpec(memory_space=pltpu.VMEM)
SMEM = pl.BlockSpec(memory_space=pltpu.SMEM)
DMA = pltpu.SemaphoreType.DMA


def places():
    return lax.axis_index("seq"), lax.axis_index("tp")


def greet(peers):
    barrier = pltpu.get_barrier_semaphore()
    for peer in peers:
        pl.semaphore_signal(barrier, inc=1, device_id=peer, device_id_type=MESH)
    pl.semaphore_wait(barrier, len(peers))


def remote(src, dst, send, recv, peer):
    return pltpu.make_async_remote_copy(
        src_ref=src, dst_ref=dst, send_sem=send, recv_sem=recv, device_id=peer, device_id_type=MESH
    )


def push(src, dst, send, recv, peer):
    copy = remote(src, dst, send, recv, peer)
    copy.start()
    return copy


def tp_peers(s, t):
    return [(s, t ^ k) for k in range(1, 8)]


def seq_peer(s, t, k, j):
    z, r = s // 4, s % 4
    return ((z + k) % 8) * 4 + (r ^ j), t


def split_matrix(n):
    row = lax.broadcasted_iota(jnp.int32, (n, n), 0)
    col = lax.broadcasted_iota(jnp.int32, (n, n), 1)
    half = n // 2
    return jnp.where(col == jnp.where(row < half, 2 * row, 2 * (row - half) + 1), 1.0, 0.0).astype(BF)


def gather_kernel(
    tok,
    qkv,
    proj,
    f_gu,
    f_down,
    s_gu,
    tok_all,
    w_all,
    f_gu_out,
    f_down_out,
    s_gu_out,
    w,
    fbuf,
    sbuf,
    lsem,
    tok_s,
    tok_r,
    x_s,
    x_r,
    z_s,
    z_r,
    c_s,
    c_r,
    p_s,
):
    s, t = places()
    z, xh, c = s // 4, (s // 2) % 2, s % 2
    up = (((z + 1) % 8) * 4 + xh * 2 + c, t)
    down = (((z + 7) % 8) * 4 + xh * 2 + c, t)
    over = (s ^ 2, t)
    twin = (s ^ 1, t)

    pulls = []
    for col in range(16):
        span = pl.ds(col * 128, 128)
        pulls.append(pltpu.make_async_copy(f_gu.at[:, :, span], fbuf.at[col], p_s.at[0, col]))
    for col in range(16):
        span = pl.ds(col * 128, 128)
        pulls.append(pltpu.make_async_copy(s_gu.at[:, :, span], sbuf.at[col], p_s.at[1, col]))
    for j in range(3):
        w[:, j * 256 : j * 256 + 256] = qkv[j].astype(BF)
    w[:, 768:1024] = proj[...].astype(BF)
    greet(tp_peers(s, t) + [up, down, over, twin])

    def block(dz, a):
        return w_all.at[(z + dz) % 8, xh ^ a, c]

    own = w.at[:, :]
    home = w_all.at[z, xh, c]
    waits = [push(own, home, x_s, x_r, over)]
    ups = {(0, 0): push(own, home, z_s.at[0, 0, 0], z_r.at[0, 0, 0], up)}
    downs = {(0, 0): push(own, home, z_s.at[1, 0, 0], z_r.at[1, 0, 0], down)}
    twins = [push(own, home, c_s.at[0, 0], c_r.at[0, 0], twin)]
    local_w = pltpu.make_async_copy(own, home, lsem.at[0])
    local_w.start()
    mine = tok_all.at[:, pl.ds(pl.multiple_of(t * 256, 256), 256)]
    local_t = pltpu.make_async_copy(tok, mine, lsem.at[1])
    local_t.start()
    toks = [push(tok, mine, tok_s.at[k], tok_r.at[k], (s, t ^ k)) for k in range(1, 8)]
    for pull in pulls:
        pull.start()

    f_flat = fbuf.reshape(16, 352, 128)
    s_flat = sbuf.reshape(16, 704, 128)

    def part_fresh(first):
        for col in range(first, first + 4):
            pulls[col].wait()
            for kind in range(2):
                f_gu_out[kind, :, col * 128 : col * 128 + 128] = f_flat[
                    col, pl.ds(kind, 176, stride=2), :
                ].astype(BF)

    def part_down():
        f_down_out[...] = f_down[...].astype(BF)

    def part_server(col):
        for pull in pulls[16 + 2 * col : 18 + 2 * col]:
            pull.wait()
        for first, count in ((0, 256), (256, 256), (512, 192)):
            half = count // 2
            pair = jnp.concatenate(
                [s_flat[2 * col + i, first : first + count, :] for i in range(2)], axis=1
            )
            split = jnp.dot(split_matrix(count), pair, preferred_element_type=F32).astype(BF)
            for kind in range(2):
                s_gu_out[kind, first // 2 : first // 2 + half, col * 256 : col * 256 + 256] = split[
                    kind * half : kind * half + half
                ]

    work = [functools.partial(part_fresh, 4 * i) for i in range(4)] + [part_down]
    work += [functools.partial(part_server, col) for col in range(8)]

    waits[0].wait_recv()
    theirs = block(0, 1)
    ups[(0, 1)] = push(theirs, theirs, z_s.at[0, 0, 1], z_r.at[0, 0, 1], up)
    downs[(0, 1)] = push(theirs, theirs, z_s.at[1, 0, 1], z_r.at[1, 0, 1], down)
    twins.append(push(theirs, theirs, c_s.at[0, 1], c_r.at[0, 1], twin))

    for step in range(4):
        for a in range(2):
            for way, (chain, peer, dz) in enumerate(((ups, up, -1 - step), (downs, down, 1 + step))):
                if (step, a) not in chain:
                    continue
                if work:
                    work.pop(0)()
                chain[(step, a)].wait_recv()
                here = block(dz + 8, a)
                if step < 2 or (step == 2 and a == way):
                    chain[(step + 1, a)] = push(
                        here, here, z_s.at[way, step + 1, a], z_r.at[way, step + 1, a], peer
                    )
                place = (dz + 8) % 8
                twins.append(push(here, here, c_s.at[place, a], c_r.at[place, a], twin))
    for piece in work:
        piece()
    for copy in twins + toks:
        copy.wait()
    for copy in list(ups.values()) + list(downs.values()) + waits:
        copy.wait_send()
    local_w.wait()
    local_t.wait()


def gather(tok, qkv, proj, f_gu, f_down, s_gu):
    return pl.pallas_call(
        gather_kernel,
        out_shape=(
            jax.ShapeDtypeStruct((256, 2048), BF),
            jax.ShapeDtypeStruct((8, 2, 2, 64, 1024), BF),
            jax.ShapeDtypeStruct((2, 176, 2048), BF),
            jax.ShapeDtypeStruct((176, 2048), BF),
            jax.ShapeDtypeStruct((2, 352, 2048), BF),
        ),
        in_specs=[VMEM, VMEM, VMEM, ANY, VMEM, ANY],
        out_specs=(VMEM,) * 5,
        scratch_shapes=[
            pltpu.VMEM((64, 1024), BF),
            pltpu.VMEM((16, 176, 2, 128), F32),
            pltpu.VMEM((16, 352, 2, 128), BF),
            DMA((2,)),
            DMA((8,)),
            DMA((8,)),
            DMA,
            DMA,
            DMA((2, 4, 2)),
            DMA((2, 4, 2)),
            DMA((8, 2)),
            DMA((8, 2)),
            DMA((2, 16)),
        ],
        compiler_params=pltpu.CompilerParams(
            collective_id=0, has_side_effects=True, vmem_limit_bytes=28 << 20
        ),
        name="gather_inputs",
    )(tok, qkv, proj, f_gu, f_down, s_gu)


def nt(a, b):
    return lax.dot_general(a, b, (((1,), (1,)), ((), ())), preferred_element_type=F32)


def attention_kernel(
    tok, w, gain, cosf, sinf, limit, cache, out, buf, vals, scores, top, total, acc, xn, sem
):
    chunks, width = 8, 512

    def fetch(i, h):
        rows = pl.ds(pl.multiple_of(i * width, width), width)
        return pltpu.make_async_copy(
            cache.at[rows, :, pl.ds(h * 128, 128)], buf.at[h, rows], sem.at[i, h]
        )

    for i in range(chunks):
        for h in range(2):
            fetch(i, h).start()
    field = tok[...].astype(F32)
    inv = lax.rsqrt(jnp.mean(field * field, axis=-1, keepdims=True) + 1e-6)
    xn[...] = (field * inv * gain[...]).astype(BF)
    projected = jnp.dot(xn[...], w[:, 0:768], preferred_element_type=F32)

    def turned(part):
        return (part * cosf[...] + pltpu.roll(part, 64, 1) * sinf[...]).astype(BF)

    queries = [turned(projected[:, h * 128 : h * 128 + 128]) for h in range(2)]
    keys_new = [turned(projected[:, 256 + h * 128 : 384 + h * 128]) for h in range(2)]
    values_new = [projected[:, 512 + h * 128 : 640 + h * 128].astype(BF) for h in range(2)]
    perm = split_matrix(256)
    row_id = lax.broadcasted_iota(jnp.int32, (256, width), 0)
    flat = [buf.at[h].reshape(8192, 128) for h in range(2)]

    new_row = lax.broadcasted_iota(jnp.int32, (256, 256), 0)
    new_col = lax.broadcasted_iota(jnp.int32, (256, 256), 1)
    for h in range(2):
        fresh = jnp.where(new_col <= new_row, nt(queries[h], keys_new[h]), -1e30)
        scores[h, chunks, :, 0:256] = fresh
        top[h] = jnp.maximum(fresh[:, 0:128], fresh[:, 128:256])

    @pl.loop(0, chunks)
    def _(i):
        for h in range(2):
            fetch(i, h).wait()
        keys = [[], []]
        for part in range(4):
            start = pl.multiple_of(i * 1024 + part * 256, 256)
            both = jnp.concatenate([flat[h][pl.ds(start, 256), :] for h in range(2)], axis=1)
            split = jnp.dot(perm, both, preferred_element_type=F32).astype(BF)
            spot = pl.multiple_of(i * width + part * 128, 128)
            vals[pl.ds(spot, 128), :] = split[128:256]
            for h in range(2):
                keys[h].append(split[0:128, h * 128 : h * 128 + 128])
        seen = row_id < limit[:, pl.ds(pl.multiple_of(i * width, width), width)]
        for h in range(2):
            key_block = jnp.concatenate(keys[h], axis=0)
            block = jnp.where(seen, nt(queries[h], key_block), -1e30)
            scores[h, i] = block
            peak = jnp.maximum(
                jnp.maximum(block[:, 0:128], block[:, 128:256]),
                jnp.maximum(block[:, 256:384], block[:, 384:512]),
            )
            top[h] = jnp.maximum(top[h], peak)

    scale = 1.4426950408889634 / (HEAD_DIM**0.5)
    for h in range(2):
        top[h] = jnp.broadcast_to(jnp.max(top[h], axis=1, keepdims=True), (256, 128))
        peak = top[h]
        weights = jnp.exp2((scores[h, chunks, :, 0:256] - jnp.tile(peak, (1, 2))) * scale)
        total[h] = weights[:, 0:128] + weights[:, 128:256]
        acc[h] = jnp.dot(weights.astype(BF), values_new[h], preferred_element_type=F32)

    @pl.loop(0, chunks)
    def _(i):
        for h in range(2):
            weights = jnp.exp2((scores[h, i] - jnp.tile(top[h], (1, 4))) * scale)
            total[h] += (weights[:, 0:128] + weights[:, 128:256]) + (
                weights[:, 256:384] + weights[:, 384:512]
            )
            spots = pl.ds(pl.multiple_of(i * width, width), width)
            acc[h] += jnp.dot(
                weights.astype(BF), vals[spots, h * 128 : h * 128 + 128], preferred_element_type=F32
            )

    mixed = jnp.concatenate(
        [(acc[h] / jnp.sum(total[h], axis=1, keepdims=True)).astype(BF) for h in range(2)], axis=1
    )
    for part in range(8):
        out[part] = nt(mixed, w[part * 256 : part * 256 + 256, 768:1024]).astype(BF)


def attention(tok, w, gain, cosf, sinf, limit, cache):
    return pl.pallas_call(
        attention_kernel,
        out_shape=jax.ShapeDtypeStruct((8, 256, 256), BF),
        in_specs=[VMEM] * 6 + [ANY],
        out_specs=VMEM,
        scratch_shapes=[
            pltpu.VMEM((2, 4096, 2, 128), BF),
            pltpu.VMEM((4096, 256), BF),
            pltpu.VMEM((2, 9, 256, 512), F32),
            pltpu.VMEM((2, 256, 128), F32),
            pltpu.VMEM((2, 256, 128), F32),
            pltpu.VMEM((2, 256, 128), F32),
            pltpu.VMEM((256, 2048), BF),
            DMA((8, 2)),
        ],
        compiler_params=pltpu.CompilerParams(vmem_limit_bytes=30 << 20),
        name="attention",
    )(tok, w, gain, cosf, sinf, limit, cache)


def scatter_sum_kernel(part, got, lsem, ssem, rsem):
    s, t = places()
    greet(tp_peers(s, t))
    local = pltpu.make_async_copy(part.at[t], got.at[t], lsem)
    local.start()
    copies = [push(part.at[t ^ k], got.at[t], ssem.at[k], rsem.at[k], (s, t ^ k)) for k in range(1, 8)]
    for copy in copies:
        copy.wait()
    local.wait()


def scatter_sum(part):
    return pl.pallas_call(
        scatter_sum_kernel,
        out_shape=jax.ShapeDtypeStruct((8, 256, 256), BF),
        in_specs=[VMEM],
        out_specs=VMEM,
        scratch_shapes=[DMA, DMA((8,)), DMA((8,))],
        compiler_params=pltpu.CompilerParams(collective_id=1, has_side_effects=True),
        name="project_exchange",
    )(part)


def slot_rows(rank, first):
    shelf = lax.broadcasted_iota(jnp.int32, (32, 256), 0).astype(F32)
    return [jnp.where(rank[first + e : first + e + 1, :] == shelf, 1.0, 0.0) for e in range(8)]


def send_rows_kernel(got, tok, rank, routes, router, gain, hidden, rows, stats):
    total = tok[...].astype(F32)
    part = got[0].astype(F32)
    for k in range(1, 8):
        part += got[k].astype(F32)
    state = (total + part).astype(BF)
    hidden[...] = state
    for chunk in range(8):
        pick = jnp.concatenate(slot_rows(rank, chunk * 8), axis=0).astype(BF)
        rows[chunk] = jnp.dot(pick, state, preferred_element_type=F32).astype(BF)
    wide = state.astype(F32)
    logits = nt(router[...], (wide * gain[...]).astype(BF))
    expert = lax.broadcasted_iota(jnp.int32, (64, 256), 0)
    lines = [
        jnp.sum(jnp.where(routes[k : k + 1, :] == expert, logits, 0.0), axis=0, keepdims=True)
        for k in range(6)
    ]
    square = jnp.sum(jnp.transpose(wide * wide), axis=0, keepdims=True)
    stats[...] = jnp.concatenate(lines + [square, jnp.zeros((1, 256), F32)], axis=0)


def send_rows(got, tok, rank, routes, router, gain):
    return pl.pallas_call(
        send_rows_kernel,
        out_shape=(
            jax.ShapeDtypeStruct((256, 256), BF),
            jax.ShapeDtypeStruct((8, 256, 256), BF),
            jax.ShapeDtypeStruct((8, 256), F32),
        ),
        in_specs=[VMEM] * 6,
        out_specs=(VMEM,) * 3,
        name="send_rows",
    )(got, tok, rank, routes, router, gain)


def moe_kernel(
    rows,
    stats,
    flag,
    gain,
    s_gu,
    s_down,
    a_gu,
    a_down,
    b_gu,
    b_down,
    back,
    stats_all,
    stage,
    xstage,
    x,
    y,
    ybuf,
    halves,
    xbuf,
    sums,
    w_gu,
    w_down,
    lsem,
    g_s,
    g_r,
    d_s,
    d_r,
    dx_s,
    dx_r,
    dy_s,
    dy_r,
    ry_s,
    ry_r,
    rx_s,
    rx_r,
    r_s,
    r_r,
):
    s, t = places()
    z, r = s // 4, s % 4
    side, mine = t // 4, t % 2
    cross = (s, t ^ 4)
    far = [seq_peer(s, t, k, j) for k in range(8) for j in range(4) if (k, j) != (0, 0)]
    greet(tp_peers(s, t) + far)

    def distance(i):
        return jnp.where(i % 2 == 1, (i + 1) // 2, (8 - i // 2) % 8)

    def arriving(i, j):
        source = ((z + 8 - distance(i)) % 8) * 4 + (r ^ j)
        return remote(rows.at[:, source], stage.at[:, source], d_s.at[i, j], d_r.at[i, j], (s, t ^ 1))

    def leaving(i, j):
        target = ((z + distance(i)) % 8) * 4 + (r ^ j)
        return remote(rows.at[:, target], stage.at[:, s], d_s.at[i, j], d_r.at[i, j], (target, t))

    def group(i):
        return pl.ds(((z + 8 - distance(i)) % 8) * 4, 4)

    def crossing(i):
        here = group(i)
        return remote(stage.at[:, here], xstage.at[:, here], dx_s.at[i], dx_r.at[i], cross)

    def columns(which):
        owner = t ^ (4 * which)
        return pl.ds(pl.multiple_of(owner * 256, 256), 256)

    def spreading(i, which, m):
        here = group(i)
        buf = (stage, xstage)[which]
        return remote(
            buf.at[(t ^ m) % 2, here],
            x.at[here, :, columns(which)],
            dy_s.at[i, which, m],
            dy_r.at[i, which, m],
            (s, t ^ m),
        )

    def keeping(i, which):
        here = group(i)
        buf = (stage, xstage)[which]
        return pltpu.make_async_copy(
            buf.at[mine, here], x.at[here, :, columns(which)], dy_s.at[i, which, 0]
        )

    def sharing(i, m):
        here = group(i)
        return remote(
            y.at[:, (t ^ m) % 4, here], ybuf.at[m - 1, :, here], ry_s.at[i, m], ry_r.at[i, m], (s, t ^ m)
        )

    def joining(i):
        here = group(i)
        return remote(halves.at[1 - side, :, here], xbuf.at[:, here], rx_s.at[i], rx_r.at[i], cross)

    def returning(i, j):
        target = ((z + 8 - distance(i)) % 8) * 4 + (r ^ j)
        return remote(sums.at[:, target], back.at[:, s], r_s.at[i, j], r_r.at[i, j], (target, t))

    own_in = pltpu.make_async_copy(rows.at[:, s], stage.at[:, s], lsem.at[0])
    own_out = pltpu.make_async_copy(sums.at[:, s], back.at[:, s], lsem.at[1])
    own_in.start()
    for j in range(1, 4):
        leaving(0, j).start()

    @pl.loop(1, 8)
    def _(i):
        for j in range(4):
            leaving(i, j).start()

    def statistics(k):
        return remote(stats, stats_all.at[t], g_s.at[k], g_r.at[k], (s, t ^ k))

    near = pltpu.make_async_copy(stats, stats_all.at[t], lsem.at[2])
    near.start()
    for k in range(1, 8):
        statistics(k).start()

    chosen = flag[...] > 0.0

    def choose(mask, new, old):
        return jnp.where(mask, new, old)

    for first, gu, down in ((mine * 176, a_gu, a_down), (176 - mine * 176, b_gu, b_down)):

        @pl.loop(0, 11)
        def _(i):
            here = pl.ds(pl.multiple_of(i * 16, 16), 16)
            there = pl.ds(pl.multiple_of(first + i * 16, 16), 16)
            for kind in range(2):
                w_gu[kind, there, :] = choose(
                    chosen, gu[kind, here, :].astype(F32), s_gu[kind, there, :].astype(F32)
                ).astype(BF)
            w_down[there, :] = choose(
                chosen, down[here, :].astype(F32), s_down[there, :].astype(F32)
            ).astype(BF)

    def arrive(i):
        @pl.when(i == 0)
        def _():
            own_in.wait()

        @pl.when(i > 0)
        def _():
            arriving(i, 0).wait_recv()

        for j in range(1, 4):
            arriving(i, j).wait_recv()
        crossing(i).start()
        for m in range(1, 4):
            spreading(i, 0, m).start()
        keeping(i, 0).start()

    def spread(i):
        crossing(i).wait_recv()
        for m in range(1, 4):
            spreading(i, 1, m).start()
        keeping(i, 1).start()

    def compute(i):
        for which in range(2):
            for m in range(1, 4):
                spreading(i, which, m).wait_recv()
            keeping(i, which).wait()
        here = group(i)
        field = x[here].reshape(128, 2048).astype(F32)
        inv = lax.rsqrt(jnp.mean(field * field, axis=-1, keepdims=True) + 1e-6)
        block = (field * inv * gain[...]).astype(BF)
        gate = nt(block, w_gu[0])
        lift = nt(block, w_gu[1])
        act = (gate / (1.0 + jnp.exp(-gate)) * lift).astype(BF)
        for part in range(8):
            result = jnp.dot(
                act, w_down[:, part * 256 : part * 256 + 256], preferred_element_type=F32
            )
            y[part // 4, part % 4, here] = result.astype(BF).reshape(4, 32, 256)
        for m in range(1, 4):
            sharing(i, m).start()

    def fold(i):
        here = group(i)
        for m in range(1, 4):
            sharing(i, m).wait_recv()
        for col in range(2):
            same = y[col, t % 4, here].astype(F32) + ybuf[1, col, here].astype(F32)
            halves[col, mine, here] = same.astype(BF)
            other = ybuf[0, col, here].astype(F32) + ybuf[2, col, here].astype(F32)
            halves[col, 1 - mine, here] = other.astype(BF)
        joining(i).start()

    def finish(i):
        here = group(i)
        joining(i).wait_recv()
        for par in range(2):
            total = halves[side, par, here].astype(F32) + xbuf[par, here].astype(F32)
            sums[par, here] = total.astype(BF)

        @pl.when(i == 0)
        def _():
            own_out.start()

        @pl.when(i > 0)
        def _():
            returning(i, 0).start()

        for j in range(1, 4):
            returning(i, j).start()

    @pl.loop(0, 12)
    def _(i):
        for lag, stage_of in enumerate((arrive, spread, compute, fold, finish)):

            @pl.when((i >= lag) & (i < lag + 8))
            def _():
                stage_of(i - lag)

    own_out.wait()
    near.wait()
    for k in range(1, 8):
        statistics(k).wait()

    def settle(i, j):
        leaving(i, j).wait_send()
        returning(i, j).wait()

    for j in range(1, 4):
        settle(0, j)

    @pl.loop(1, 8)
    def _(i):
        for j in range(4):
            settle(i, j)

    @pl.loop(0, 8)
    def _(i):
        crossing(i).wait_send()
        joining(i).wait_send()
        for m in range(1, 4):
            sharing(i, m).wait_send()
            for which in range(2):
                spreading(i, which, m).wait_send()


def moe(*operands):
    return pl.pallas_call(
        moe_kernel,
        out_shape=(
            jax.ShapeDtypeStruct((2, 32, 32, 256), BF),
            jax.ShapeDtypeStruct((8, 8, 256), F32),
        ),
        in_specs=[VMEM] * 10,
        out_specs=(VMEM, VMEM),
        scratch_shapes=[
            pltpu.VMEM((2, 32, 32, 256), BF),
            pltpu.VMEM((2, 32, 32, 256), BF),
            pltpu.VMEM((32, 32, 2048), BF),
            pltpu.VMEM((2, 4, 32, 32, 256), BF),
            pltpu.VMEM((3, 2, 32, 32, 256), BF),
            pltpu.VMEM((2, 2, 32, 32, 256), BF),
            pltpu.VMEM((2, 32, 32, 256), BF),
            pltpu.VMEM((2, 32, 32, 256), BF),
            pltpu.VMEM((2, 352, 2048), BF),
            pltpu.VMEM((352, 2048), BF),
            DMA((3,)),
            DMA((8,)),
            DMA((8,)),
            DMA((8, 4)),
            DMA((8, 4)),
            DMA((8,)),
            DMA((8,)),
            DMA((8, 2, 4)),
            DMA((8, 2, 4)),
            DMA((8, 4)),
            DMA((8, 4)),
            DMA((8,)),
            DMA((8,)),
            DMA((8, 4)),
            DMA((8, 4)),
        ],
        compiler_params=pltpu.CompilerParams(
            collective_id=2, has_side_effects=True, vmem_limit_bytes=48 << 20
        ),
        name="moe",
    )(*operands)


def combine_kernel(back, hidden, rank, routes, stats, out):
    lines = stats[0]
    for k in range(1, 8):
        lines += stats[k]
    inv = lax.rsqrt(lines[6:7, :] * (1.0 / 2048.0) + 1e-6)
    gate = 1.0 / (1.0 + jnp.exp(-(lines * inv)))
    shelf = lax.broadcasted_iota(jnp.int32, (64, 256), 0)
    expert = (shelf % 32) * 2 + shelf // 32
    share = jnp.zeros((64, 256), F32)
    for k in range(6):
        share += jnp.where(routes[k : k + 1, :] == expert, gate[k : k + 1, :], 0.0)
    total = hidden[...].astype(F32)
    for chunk in range(8):
        pick = slot_rows(rank, chunk * 8)
        mix = jnp.concatenate(
            [pick[e] * share[chunk * 8 + e : chunk * 8 + e + 1, :] for e in range(8)], axis=0
        )
        high = mix.astype(BF)
        low = (mix - high.astype(F32)).astype(BF)
        dims = (((0,), (0,)), ((), ()))
        total += lax.dot_general(high, back[chunk], dims, preferred_element_type=F32)
        total += lax.dot_general(low, back[chunk], dims, preferred_element_type=F32)
    out[...] = total.astype(BF)


def combine(back, hidden, rank, routes, stats):
    return pl.pallas_call(
        combine_kernel,
        out_shape=jax.ShapeDtypeStruct((256, 256), BF),
        in_specs=[VMEM] * 5,
        out_specs=VMEM,
        name="combine",
    )(back, hidden, rank, routes, stats)


def swapped(array):
    return lax.ppermute(array, "tp", [(i, i ^ 1) for i in range(8)])


def body(
    tokens,
    ctx_len,
    cache_kv,
    cache_pos,
    attn_gain,
    moe_gain,
    qkv_train,
    out_train,
    router,
    routes,
    handed_half,
    fresh_gu,
    fresh_down,
    server_gu,
    server_down,
):
    t = lax.axis_index("tp")
    s = lax.axis_index("seq")
    tok_all, w_all, own_gu, own_down, serve_gu = gather(
        tokens,
        qkv_train.transpose(1, 0, 2),
        out_train,
        fresh_gu[0],
        fresh_down[0],
        server_gu[0],
    )
    other_gu, other_down = swapped((own_gu, own_down))

    context = ctx_len[0]
    half = HEAD_DIM // 2
    frequency = 10000.0 ** (-jnp.arange(half, dtype=F32) / half)
    positions = context + jnp.arange(256, dtype=jnp.int32)
    angles = positions.astype(F32)[:, None] * frequency[None, :]
    cosine, sine = jnp.cos(angles), jnp.sin(angles)
    cosf = jnp.concatenate([cosine, cosine], axis=1)
    sinf = jnp.concatenate([-sine, sine], axis=1)
    slot = cache_pos
    limit = jnp.where(slot < 0, 0, jnp.where(slot < SINK, 256, slot + WIN - context))
    part = attention(
        tok_all,
        w_all.reshape(2048, 1024),
        attn_gain.reshape(1, 2048),
        cosf,
        sinf,
        limit,
        cache_kv[0],
    )
    got = scatter_sum(part)

    routes_t = routes.T
    shelf = jnp.arange(64, dtype=jnp.int32)
    named = (shelf % 32) * 2 + shelf // 32
    hit = jnp.any(routes_t[None, :, :] == named[:, None, None], axis=1)
    later = (jnp.arange(256)[:, None] < jnp.arange(256)[None, :]).astype(BF)
    before = jnp.dot(hit.astype(BF), later, preferred_element_type=F32)
    rank = jnp.where(hit, before, -1.0)

    columns = t * 256
    gain_part = lax.dynamic_slice_in_dim(moe_gain, columns, 256, 0).reshape(1, 256)
    router_part = lax.dynamic_slice_in_dim(router, columns, 256, 0).T
    hidden, rows, stats = send_rows(got, tokens, rank, routes_t, router_part, gain_part)
    parity = t % 2
    use_fresh = lax.dynamic_index_in_dim(handed_half, s, 0, keepdims=False) == parity
    flag = jnp.broadcast_to(use_fresh.astype(F32), (1, 2048))
    back, stats_all = moe(
        rows.reshape(2, 32, 32, 256),
        stats,
        flag,
        moe_gain.reshape(1, 2048),
        serve_gu,
        server_down[0],
        own_gu,
        own_down,
        other_gu,
        other_down,
    )
    return combine(back.reshape(8, 256, 256), hidden, rank, routes_t, stats_all)


def solution(mesh):
    placed = (
        P("seq", "tp"),
        P("seq"),
        P("seq", None, None, "tp"),
        P("seq", None),
        P(),
        P(),
        P("seq", None, "tp"),
        P("seq", "tp"),
        P(),
        P("seq", None),
        P(),
        P("seq", "tp", None, None),
        P("seq", "tp", None),
        P("seq", "tp", None, None),
        P("seq", "tp", None),
    )
    return jax.shard_map(
        body, mesh=mesh, in_specs=placed, out_specs=P("seq", "tp"), check_vma=False
    )
```

```python
import functools

import jax
import jax.numpy as jnp
from jax import lax
from jax.experimental import pallas as pl
from jax.experimental.pallas import tpu as pltpu
from jax.sharding import PartitionSpec as P

HEAD_DIM = 128
SINK = 4
WIN = 4096
MESH = pl.DeviceIdType.MESH
BF = jnp.bfloat16
F32 = jnp.float32
ANY = pl.BlockSpec(memory_space=pl.ANY)
VMEM = pl.BlockSpec(memory_space=pltpu.VMEM)
SMEM = pl.BlockSpec(memory_space=pltpu.SMEM)
DMA = pltpu.SemaphoreType.DMA


def places():
    return lax.axis_index("seq"), lax.axis_index("tp")


def greet(peers):
    barrier = pltpu.get_barrier_semaphore()
    for peer in peers:
        pl.semaphore_signal(barrier, inc=1, device_id=peer, device_id_type=MESH)
    pl.semaphore_wait(barrier, len(peers))


def remote(src, dst, send, recv, peer):
    return pltpu.make_async_remote_copy(
        src_ref=src, dst_ref=dst, send_sem=send, recv_sem=recv, device_id=peer, device_id_type=MESH
    )


def push(src, dst, send, recv, peer):
    copy = remote(src, dst, send, recv, peer)
    copy.start()
    return copy


def tp_peers(s, t):
    return [(s, t ^ k) for k in range(1, 8)]


def seq_peer(s, t, k, j):
    z, r = s // 4, s % 4
    return ((z + k) % 8) * 4 + (r ^ j), t


def split_matrix(n):
    row = lax.broadcasted_iota(jnp.int32, (n, n), 0)
    col = lax.broadcasted_iota(jnp.int32, (n, n), 1)
    half = n // 2
    return jnp.where(col == jnp.where(row < half, 2 * row, 2 * (row - half) + 1), 1.0, 0.0).astype(BF)


def nt(a, b):
    return lax.dot_general(a, b, (((1,), (1,)), ((), ())), preferred_element_type=F32)


def slot_rows(rank, first):
    shelf = lax.broadcasted_iota(jnp.int32, (32, 256), 0).astype(F32)
    return [jnp.where(rank[first + e : first + e + 1, :] == shelf, 1.0, 0.0) for e in range(8)]


CHUNKS, WIDTH = 8, 512


def layer_kernel(
    tok,
    context,
    handed,
    qkv,
    proj,
    f_gu,
    f_down,
    s_gu,
    s_down,
    gain,
    moe_gain,
    cosine,
    sine,
    slots,
    cache,
    routes,
    router,
    out,
    hidden,
    rows,
    stats,
    s_gu_out,
    f_gu_out,
    f_down_out,
    o_gu_out,
    o_down_out,
    rank,
    share,
    final,
    wq,
    wo,
    wq_all,
    wo_all,
    tok_all,
    part,
    got,
    qbuf,
    pbuf,
    fbuf,
    sbuf,
    cbuf,
    scores,
    top,
    total,
    acc,
    xn,
    back,
    stats_all,
    stage,
    xstage,
    x,
    y,
    ybuf,
    halves,
    xbuf,
    sums,
    w_down,
    lsem,
    fsem,
    ssem,
    csem,
    tok_s,
    tok_r,
    swap_s,
    swap_r,
    x_s,
    x_r,
    z_s,
    z_r,
    c_s,
    c_r,
    p_s,
    p_r,
    g_s,
    g_r,
    d_s,
    d_r,
    dx_s,
    dx_r,
    dy_s,
    dy_r,
    ry_s,
    ry_r,
    rx_s,
    rx_r,
    r_s,
    r_r,
):
    s, t = places()
    z, xh, c = s // 4, (s // 2) % 2, s % 2
    up = (((z + 1) % 8) * 4 + xh * 2 + c, t)
    down = (((z + 7) % 8) * 4 + xh * 2 + c, t)
    over = (s ^ 2, t)
    twin = (s ^ 1, t)

    pull_q = pltpu.make_async_copy(qkv, qbuf, lsem.at[0])
    pull_p = pltpu.make_async_copy(proj, pbuf, lsem.at[1])
    pull_d = [
        pltpu.make_async_copy(
            f_down.at[:, pl.ds(i * 512, 512)], scores.at[0, i, pl.ds(0, 176)], lsem.at[10 + i]
        )
        for i in range(4)
    ]
    pull_w = pltpu.make_async_copy(s_down, w_down, lsem.at[6])
    pull_q.start()
    pull_p.start()
    for pull in pull_d:
        pull.start()
    f_pulls, s_pulls = [], []
    for col in range(16):
        span = pl.ds(col * 128, 128)
        f_pulls.append(pltpu.make_async_copy(f_gu.at[:, :, span], fbuf.at[col], fsem.at[col]))
        s_pulls.append(pltpu.make_async_copy(s_gu.at[:, :, span], sbuf.at[col], ssem.at[col]))
    for pull in f_pulls:
        pull.start()

    def fetch(i, h):
        span = pl.ds(pl.multiple_of(i * WIDTH, WIDTH), WIDTH)
        return pltpu.make_async_copy(
            cache.at[span, :, pl.ds(h * 128, 128)], cbuf.at[h, span], csem.at[i, h]
        )

    far = [seq_peer(s, t, k, j) for k in range(8) for j in range(4) if (k, j) != (0, 0)]
    greet(tp_peers(s, t) + far)
    spot = tok_all.at[:, pl.ds(pl.multiple_of(t * 256, 256), 256)]
    toks = [push(tok, spot, tok_s.at[k], tok_r.at[k], (s, t ^ k)) for k in range(1, 8)]
    local_t = pltpu.make_async_copy(tok, spot, lsem.at[3])
    local_t.start()
    pull_q.wait()
    for j in range(3):
        wq[:, j * 256 : j * 256 + 256] = qbuf[j].astype(BF)

    class Ring:
        def __init__(self, own, whole, which):
            self.own, self.whole, self.which = own, whole, which
            self.ups, self.downs, self.twins = {}, {}, []

        def block(self, dz, a):
            return self.whole.at[(z + dz + 8) % 8, xh ^ a, c]

        def pass_on(self, src, dst, step, a, ways):
            for way, chain, peer in ((0, self.ups, up), (1, self.downs, down)):
                if way in ways:
                    at = (self.which, way, step, a)
                    chain[(step, a)] = push(src, dst, z_s.at[at], z_r.at[at], peer)

        def to_twin(self, src, dst, place, a):
            at = (self.which, place, a)
            self.twins.append(push(src, dst, c_s.at[at], c_r.at[at], twin))

        def begin(self):
            home = self.block(0, 0)
            self.across = push(self.own, home, x_s.at[self.which], x_r.at[self.which], over)
            self.pass_on(self.own, home, 0, 0, (0, 1))
            self.to_twin(self.own, home, 0, 0)
            self.local = pltpu.make_async_copy(self.own, home, lsem.at[4 + self.which])
            self.local.start()

        def partner(self):
            self.across.wait_recv()
            theirs = self.block(0, 1)
            self.pass_on(theirs, theirs, 0, 1, (0, 1))
            self.to_twin(theirs, theirs, 0, 1)

        def turn(self, step, a, way):
            chain = (self.ups, self.downs)[way]
            if (step, a) not in chain:
                return
            chain[(step, a)].wait_recv()
            dz = (-1 - step, 1 + step)[way]
            here = self.block(dz, a)
            if step < 2 or (step == 2 and a == way):
                self.pass_on(here, here, step + 1, a, (way,))
            self.to_twin(here, here, dz % 8, a)

        def step(self, step):
            for a in range(2):
                for way in range(2):
                    self.turn(step, a, way)

        def arrive(self):
            for copy in self.twins:
                copy.wait_recv()
            self.local.wait()

        def end(self):
            self.across.wait_send()
            for copy in self.twins + list(self.ups.values()) + list(self.downs.values()):
                copy.wait_send()

    ring_q = Ring(wq.at[:, :], wq_all, 0)
    ring_o = Ring(wo.at[:, :], wo_all, 1)
    ring_q.begin()

    f_flat = fbuf.reshape(16, 352, 128)
    s_flat = sbuf.reshape(16, 704, 128)
    c_flat = [cbuf.at[h].reshape(8192, 128) for h in range(2)]
    keys, vals = y.at[0].reshape(4096, 256), y.at[1].reshape(4096, 256)
    swaps = []

    def swap(src, dst):
        i = len(swaps)
        swaps.append(push(src, dst, swap_s.at[i], swap_r.at[i], (s, t ^ 1)))

    def part_fresh():
        for col in range(16):
            f_pulls[col].wait()
            for kind in range(2):
                f_gu_out[kind, :, col * 128 : col * 128 + 128] = f_flat[
                    col, pl.ds(kind, 176, stride=2), :
                ].astype(BF)
        for kind in range(2):
            swap(f_gu_out.at[kind], o_gu_out.at[kind])
        for i in range(CHUNKS):
            for h in range(2):
                fetch(i, h).start()

    def part_down():
        for i in range(4):
            pull_d[i].wait()
            f_down_out[:, i * 512 : i * 512 + 512] = scores[0, i, 0:176].astype(BF)
        for pull in s_pulls:
            pull.start()
        pull_w.start()
        pull_p.wait()
        wo[...] = pbuf[...].astype(BF)

    def part_cache(i):
        for h in range(2):
            fetch(i, h).wait()
        perm = split_matrix(256)
        for k in range(4):
            start = i * 1024 + k * 256
            both = jnp.concatenate([c_flat[h][start : start + 256, :] for h in range(2)], axis=1)
            split = jnp.dot(perm, both, preferred_element_type=F32).astype(BF)
            spot = i * WIDTH + k * 128
            keys[spot : spot + 128, :] = split[0:128]
            vals[spot : spot + 128, :] = split[128:256]

    def part_server(col):
        for pull in s_pulls[2 * col : 2 + 2 * col]:
            pull.wait()
        for first, count in ((0, 256), (256, 256), (512, 192)):
            half = count // 2
            pair = jnp.concatenate(
                [s_flat[2 * col + i, first : first + count, :] for i in range(2)], axis=1
            )
            split = jnp.dot(split_matrix(count), pair, preferred_element_type=F32).astype(BF)
            for kind in range(2):
                s_gu_out[kind, first // 2 : first // 2 + half, col * 256 : col * 256 + 256] = split[
                    kind * half : kind * half + half
                ]

    def part_norm():
        for copy in toks:
            copy.wait_recv()
        local_t.wait()
        field = tok_all[...].astype(F32)
        inv = lax.rsqrt(jnp.mean(field * field, axis=-1, keepdims=True) + 1e-6)
        xn[...] = (field * inv * gain[...]).astype(BF)

    def part_rank():
        shelf = lax.broadcasted_iota(jnp.int32, (64, 256), 0)
        named = (shelf % 32) * 2 + shelf // 32
        hit = jnp.zeros((64, 256), F32)
        for k in range(6):
            hit += jnp.where(routes[k : k + 1, :] == named, 1.0, 0.0)
        row = lax.broadcasted_iota(jnp.int32, (256, 256), 0)
        col = lax.broadcasted_iota(jnp.int32, (256, 256), 1)
        later = jnp.where(row < col, 1.0, 0.0).astype(BF)
        before = jnp.dot(hit.astype(BF), later, preferred_element_type=F32)
        rank[...] = jnp.where(hit > 0.0, before, -1.0)

    work = [functools.partial(part_cache, i) for i in range(8)] + [part_rank]
    work += [functools.partial(part_server, col) for col in range(2)]
    work += [part_norm]
    work += [functools.partial(part_server, col) for col in range(2, 8)]
    part_fresh()
    ring_q.partner()
    part_down()
    for step in range(4):
        for a in range(2):
            for way in range(2):
                ring_q.turn(step, a, way)
                if work:
                    work.pop(0)()
    ring_o.begin()
    for piece in work:
        piece()
    ring_o.partner()
    ring_q.arrive()

    projected = jnp.dot(xn[...], wq_all[...].reshape(2048, 768), preferred_element_type=F32)
    ring_o.step(0)

    cosf = jnp.concatenate([cosine[...], cosine[...]], axis=1)
    sinf = jnp.concatenate([-sine[...], sine[...]], axis=1)

    def turned(field):
        return (field * cosf + pltpu.roll(field, 64, 1) * sinf).astype(BF)

    queries = [turned(projected[:, h * 128 : h * 128 + 128]) for h in range(2)]
    keys_new = [turned(projected[:, 256 + h * 128 : 384 + h * 128]) for h in range(2)]
    values_new = [projected[:, 512 + h * 128 : 640 + h * 128].astype(BF) for h in range(2)]
    row_id = lax.broadcasted_iota(jnp.int32, (256, WIDTH), 0)
    new_row = lax.broadcasted_iota(jnp.int32, (256, 256), 0)
    new_col = lax.broadcasted_iota(jnp.int32, (256, 256), 1)
    for h in range(2):
        fresh = jnp.where(new_col <= new_row, nt(queries[h], keys_new[h]), -1e30)
        scores[h, CHUNKS, :, 0:256] = fresh
        top[h] = jnp.maximum(fresh[:, 0:128], fresh[:, 128:256])

    def score(first, last):
        @pl.loop(first, last)
        def _(i):
            span = pl.ds(pl.multiple_of(i * WIDTH, WIDTH), WIDTH)
            slot = slots[:, span]
            limit = jnp.where(slot < 0, 0, jnp.where(slot < SINK, 256, slot + WIN - context[0]))
            seen = row_id < limit
            for h in range(2):
                block = nt(queries[h], keys[span, h * 128 : h * 128 + 128])
                block = jnp.where(seen, block, -1e30)
                scores[h, i] = block
                peak = jnp.maximum(
                    jnp.maximum(block[:, 0:128], block[:, 128:256]),
                    jnp.maximum(block[:, 256:384], block[:, 384:512]),
                )
                top[h] = jnp.maximum(top[h], peak)

    score(0, 4)
    ring_o.step(1)
    score(4, 8)
    ring_o.step(2)

    scale = 1.4426950408889634 / (HEAD_DIM**0.5)
    for h in range(2):
        top[h] = jnp.broadcast_to(jnp.max(top[h], axis=1, keepdims=True), (256, 128))
        peak = top[h]
        weights = jnp.exp2((scores[h, CHUNKS, :, 0:256] - jnp.tile(peak, (1, 2))) * scale)
        total[h] = weights[:, 0:128] + weights[:, 128:256]
        acc[h] = jnp.dot(weights.astype(BF), values_new[h], preferred_element_type=F32)

    def weigh(first, last):
        @pl.loop(first, last)
        def _(i):
            for h in range(2):
                weights = jnp.exp2((scores[h, i] - jnp.tile(top[h], (1, 4))) * scale)
                total[h] += (weights[:, 0:128] + weights[:, 128:256]) + (
                    weights[:, 256:384] + weights[:, 384:512]
                )
                span = pl.ds(pl.multiple_of(i * WIDTH, WIDTH), WIDTH)
                acc[h] += jnp.dot(
                    weights.astype(BF), vals[span, h * 128 : h * 128 + 128], preferred_element_type=F32
                )

    weigh(0, 4)
    ring_o.step(3)
    weigh(4, 8)
    ring_o.arrive()
    mixed = jnp.concatenate(
        [(acc[h] / jnp.sum(total[h], axis=1, keepdims=True)).astype(BF) for h in range(2)], axis=1
    )

    gives = []
    for k in (2, 6, 1, 3, 4, 5, 7, 0):
        part[k] = nt(mixed, wo_all[t ^ k].reshape(256, 256)).astype(BF)
        if k:
            gives.append(push(part.at[k], got.at[k], p_s.at[k], p_r.at[k], (s, t ^ k)))
    swap(f_down_out, o_down_out)
    for copy in gives:
        copy.wait_recv()
    total_out = tok[...].astype(F32) + part[0].astype(F32)
    for k in range(1, 8):
        total_out += got[k].astype(F32)
    state = total_out.astype(BF)
    hidden[...] = state
    for chunk in range(8):
        pick = jnp.concatenate(slot_rows(rank, chunk * 8), axis=0).astype(BF)
        picked = jnp.dot(pick, state, preferred_element_type=F32).astype(BF)
        first = (chunk % 4) * 8
        rows[chunk // 4, first : first + 8] = picked.reshape(8, 32, 256)
    side, mine = t // 4, t % 2
    cross = (s, t ^ 4)
    r = s % 4
    def distance(i):
        return jnp.where(i % 2 == 1, (i + 1) // 2, (8 - i // 2) % 8)

    def arriving(i, j):
        source = ((z + 8 - distance(i)) % 8) * 4 + (r ^ j)
        return remote(rows.at[:, source], stage.at[:, source], d_s.at[i, j], d_r.at[i, j], (s, t ^ 1))

    def leaving(i, j):
        target = ((z + distance(i)) % 8) * 4 + (r ^ j)
        return remote(rows.at[:, target], stage.at[:, s], d_s.at[i, j], d_r.at[i, j], (target, t))

    def group(i):
        return pl.ds(((z + 8 - distance(i)) % 8) * 4, 4)

    def crossing(i):
        here = group(i)
        return remote(stage.at[:, here], xstage.at[:, here], dx_s.at[i], dx_r.at[i], cross)

    def columns(which):
        owner = t ^ (4 * which)
        return pl.ds(pl.multiple_of(owner * 256, 256), 256)

    def spreading(i, which, m):
        here = group(i)
        buf = (stage, xstage)[which]
        return remote(
            buf.at[(t ^ m) % 2, here],
            x.at[here, :, columns(which)],
            dy_s.at[i, which, m],
            dy_r.at[i, which, m],
            (s, t ^ m),
        )

    def keeping(i, which):
        here = group(i)
        buf = (stage, xstage)[which]
        return pltpu.make_async_copy(
            buf.at[mine, here], x.at[here, :, columns(which)], dy_s.at[i, which, 0]
        )

    def sharing(i, m):
        here = group(i)
        return remote(
            y.at[:, (t ^ m) % 4, here], ybuf.at[m - 1, :, here], ry_s.at[i, m], ry_r.at[i, m], (s, t ^ m)
        )

    def joining(i):
        here = group(i)
        return remote(halves.at[1 - side, :, here], xbuf.at[:, here], rx_s.at[i], rx_r.at[i], cross)

    def returning(i, j):
        target = ((z + 8 - distance(i)) % 8) * 4 + (r ^ j)
        return remote(sums.at[:, target], back.at[:, s], r_s.at[i, j], r_r.at[i, j], (target, t))

    own_in = pltpu.make_async_copy(rows.at[:, s], stage.at[:, s], lsem.at[7])
    own_out = pltpu.make_async_copy(sums.at[:, s], back.at[:, s], lsem.at[8])
    own_in.start()
    for j in range(1, 4):
        leaving(0, j).start()

    @pl.loop(1, 8)
    def _(i):
        for j in range(4):
            leaving(i, j).start()

    def statistics(k):
        return remote(stats, stats_all.at[t], g_s.at[k], g_r.at[k], (s, t ^ k))

    span = pl.ds(pl.multiple_of(t * 256, 256), 256)
    wide = state.astype(F32)
    logits = nt(router[:, span], (wide * moe_gain[:, span]).astype(BF))
    expert = lax.broadcasted_iota(jnp.int32, (64, 256), 0)
    lines = [
        jnp.sum(jnp.where(routes[k : k + 1, :] == expert, logits, 0.0), axis=0, keepdims=True)
        for k in range(6)
    ]
    square = jnp.sum(jnp.transpose(wide * wide), axis=0, keepdims=True)
    stats[...] = jnp.concatenate(lines + [square, jnp.zeros((1, 256), F32)], axis=0)
    near = pltpu.make_async_copy(stats, stats_all.at[t], lsem.at[9])
    near.start()
    for k in range(1, 8):
        statistics(k).start()

    def choose():
        for copy in swaps:
            copy.wait_recv()
        pull_w.wait()
        chosen = jnp.broadcast_to(handed[s], (16, 2048)) == mine
        for first, gu, down in (
            (mine * 176, f_gu_out, f_down_out),
            (176 - mine * 176, o_gu_out, o_down_out),
        ):

            @pl.loop(0, 11)
            def _(i):
                here = pl.ds(pl.multiple_of(i * 16, 16), 16)
                there = pl.ds(pl.multiple_of(first + i * 16, 16), 16)
                for kind in range(2):
                    s_gu_out[kind, there, :] = jnp.where(
                        chosen, gu[kind, here, :].astype(F32), s_gu_out[kind, there, :].astype(F32)
                    ).astype(BF)
                w_down[there, :] = jnp.where(
                    chosen, down[here, :].astype(F32), w_down[there, :].astype(F32)
                ).astype(BF)

    def gates():
        near.wait()
        for k in range(1, 8):
            statistics(k).wait_recv()
        sums_of = stats_all[0]
        for k in range(1, 8):
            sums_of += stats_all[k]
        inv = lax.rsqrt(sums_of[6:7, :] * (1.0 / 2048.0) + 1e-6)
        gate = 1.0 / (1.0 + jnp.exp(-(sums_of * inv)))
        shelf = lax.broadcasted_iota(jnp.int32, (64, 256), 0)
        named = (shelf % 32) * 2 + shelf // 32
        amount = jnp.zeros((64, 256), F32)
        for k in range(6):
            amount += jnp.where(routes[k : k + 1, :] == named, gate[k : k + 1, :], 0.0)
        share[...] = amount
        final[...] = hidden[...].astype(F32)

    def arrive(i):
        @pl.when(i == 0)
        def _():
            own_in.wait()

        @pl.when(i > 0)
        def _():
            arriving(i, 0).wait_recv()

        for j in range(1, 4):
            arriving(i, j).wait_recv()
        crossing(i).start()
        for m in range(1, 4):
            spreading(i, 0, m).start()
        keeping(i, 0).start()

    def spread(i):
        crossing(i).wait_recv()
        for m in range(1, 4):
            spreading(i, 1, m).start()
        keeping(i, 1).start()

    def compute(i):
        for which in range(2):
            for m in range(1, 4):
                spreading(i, which, m).wait_recv()
            keeping(i, which).wait()
        here = group(i)
        field = x[here].reshape(128, 2048).astype(F32)
        inv = lax.rsqrt(jnp.mean(field * field, axis=-1, keepdims=True) + 1e-6)
        block = (field * inv * moe_gain[...]).astype(BF)
        gate = nt(block, s_gu_out[0])
        lift = nt(block, s_gu_out[1])
        act = (gate / (1.0 + jnp.exp(-gate)) * lift).astype(BF)
        for part in range(8):
            result = jnp.dot(
                act, w_down[:, part * 256 : part * 256 + 256], preferred_element_type=F32
            )
            y[part // 4, part % 4, here] = result.astype(BF).reshape(4, 32, 256)
        for m in range(1, 4):
            sharing(i, m).start()

    def fold(i):
        here = group(i)
        for m in range(1, 4):
            sharing(i, m).wait_recv()
        for col in range(2):
            same = y[col, t % 4, here].astype(F32) + ybuf[1, col, here].astype(F32)
            halves[col, mine, here] = same.astype(BF)
            other = ybuf[0, col, here].astype(F32) + ybuf[2, col, here].astype(F32)
            halves[col, 1 - mine, here] = other.astype(BF)
        joining(i).start()

    def finish(i):
        here = group(i)
        joining(i).wait_recv()
        for par in range(2):
            total = halves[side, par, here].astype(F32) + xbuf[par, here].astype(F32)
            sums[par, here] = total.astype(BF)

        @pl.when(i == 0)
        def _():
            own_out.start()

        @pl.when(i > 0)
        def _():
            returning(i, 0).start()

        for j in range(1, 4):
            returning(i, j).start()

    def collect(i):
        @pl.when(i == 0)
        def _():
            own_out.wait()

        @pl.when(i > 0)
        def _():
            returning(i, 0).wait_recv()

        for j in range(1, 4):
            returning(i, j).wait_recv()
        first = ((z + distance(i)) % 8) * 4
        shelf = lax.broadcasted_iota(jnp.int32, (32, 256), 0).astype(F32)
        for par in range(2):
            lines = []
            for e in range(4):
                line = pl.ds(par * 32 + first + e, 1)
                lines.append(jnp.where(rank[line, :] == shelf, share[line, :], 0.0))
            mix = jnp.concatenate(lines, axis=0)
            high = mix.astype(BF)
            low = (mix - high.astype(F32)).astype(BF)
            block = back[par, pl.ds(first, 4)].reshape(128, 256)
            dims = (((0,), (0,)), ((), ()))
            final[...] += lax.dot_general(
                high, block, dims, preferred_element_type=F32
            ) + lax.dot_general(low, block, dims, preferred_element_type=F32)

    @pl.loop(0, 14)
    def _(i):
        @pl.when(i == 2)
        def _():
            choose()

        @pl.when(i == 6)
        def _():
            gates()

        for lag, stage_of in ((0, arrive), (1, spread), (2, compute), (3, fold), (4, finish), (6, collect)):

            @pl.when((i >= lag) & (i < lag + 8))
            def _():
                stage_of(i - lag)

    out[...] = final[...].astype(BF)
    for k in range(1, 8):
        statistics(k).wait_send()
    for copy in swaps + gives + toks:
        copy.wait_send()
    ring_q.end()
    ring_o.end()

    def settle(i, j):
        leaving(i, j).wait_send()
        returning(i, j).wait_send()

    for j in range(1, 4):
        settle(0, j)

    @pl.loop(1, 8)
    def _(i):
        for j in range(4):
            settle(i, j)

    @pl.loop(0, 8)
    def _(i):
        crossing(i).wait_send()
        joining(i).wait_send()
        for m in range(1, 4):
            sharing(i, m).wait_send()
            for which in range(2):
                spreading(i, which, m).wait_send()


def layer(*operands):
    return pl.pallas_call(
        layer_kernel,
        out_shape=jax.ShapeDtypeStruct((256, 256), BF),
        in_specs=[VMEM, SMEM, SMEM] + [ANY] * 6 + [VMEM] * 5 + [ANY] + [VMEM] * 2,
        out_specs=VMEM,
        scratch_shapes=[
            pltpu.VMEM((256, 256), BF),
            pltpu.VMEM((2, 32, 32, 256), BF),
            pltpu.VMEM((8, 256), F32),
            pltpu.VMEM((2, 352, 2048), BF),
            pltpu.VMEM((2, 176, 2048), BF),
            pltpu.VMEM((176, 2048), BF),
            pltpu.VMEM((2, 176, 2048), BF),
            pltpu.VMEM((176, 2048), BF),
            pltpu.VMEM((64, 256), F32),
            pltpu.VMEM((64, 256), F32),
            pltpu.VMEM((256, 256), F32),
            pltpu.VMEM((64, 768), BF),
            pltpu.VMEM((64, 256), BF),
            pltpu.VMEM((8, 2, 2, 64, 768), BF),
            pltpu.VMEM((8, 2, 2, 64, 256), BF),
            pltpu.VMEM((256, 2048), BF),
            pltpu.VMEM((8, 256, 256), BF),
            pltpu.VMEM((8, 256, 256), BF),
            pltpu.VMEM((3, 64, 256), F32),
            pltpu.VMEM((64, 256), F32),
            pltpu.VMEM((16, 176, 2, 128), F32),
            pltpu.VMEM((16, 352, 2, 128), BF),
            pltpu.VMEM((2, 4096, 2, 128), BF),
            pltpu.VMEM((2, 9, 256, 512), F32),
            pltpu.VMEM((2, 256, 128), F32),
            pltpu.VMEM((2, 256, 128), F32),
            pltpu.VMEM((2, 256, 128), F32),
            pltpu.VMEM((256, 2048), BF),
            pltpu.VMEM((2, 32, 32, 256), BF),
            pltpu.VMEM((8, 8, 256), F32),
            pltpu.VMEM((2, 32, 32, 256), BF),
            pltpu.VMEM((2, 32, 32, 256), BF),
            pltpu.VMEM((32, 32, 2048), BF),
            pltpu.VMEM((2, 4, 32, 32, 256), BF),
            pltpu.VMEM((3, 2, 32, 32, 256), BF),
            pltpu.VMEM((2, 2, 32, 32, 256), BF),
            pltpu.VMEM((2, 32, 32, 256), BF),
            pltpu.VMEM((2, 32, 32, 256), BF),
            pltpu.VMEM((352, 2048), BF),
            DMA((14,)),
            DMA((16,)),
            DMA((16,)),
            DMA((8, 2)),
            DMA((8,)),
            DMA((8,)),
            DMA((3,)),
            DMA((3,)),
            DMA((2,)),
            DMA((2,)),
            DMA((2, 2, 4, 2)),
            DMA((2, 2, 4, 2)),
            DMA((2, 8, 2)),
            DMA((2, 8, 2)),
            DMA((8,)),
            DMA((8,)),
            DMA((8,)),
            DMA((8,)),
            DMA((8, 4)),
            DMA((8, 4)),
            DMA((8,)),
            DMA((8,)),
            DMA((8, 2, 4)),
            DMA((8, 2, 4)),
            DMA((8, 4)),
            DMA((8, 4)),
            DMA((8,)),
            DMA((8,)),
            DMA((8, 4)),
            DMA((8, 4)),
        ],
        compiler_params=pltpu.CompilerParams(
            collective_id=0, has_side_effects=True, vmem_limit_bytes=60 << 20
        ),
        name="layer",
    )(*operands)


def body(
    tokens,
    ctx_len,
    cache_kv,
    cache_pos,
    attn_gain,
    moe_gain,
    qkv_train,
    out_train,
    router,
    routes,
    handed_half,
    fresh_gu,
    fresh_down,
    server_gu,
    server_down,
):
    half = HEAD_DIM // 2
    frequency = 10000.0 ** (-jnp.arange(half, dtype=F32) / half)
    positions = ctx_len[0] + jnp.arange(256, dtype=jnp.int32)
    angles = positions.astype(F32)[:, None] * frequency[None, :]
    return layer(
        tokens,
        ctx_len,
        handed_half,
        qkv_train.transpose(1, 0, 2),
        out_train,
        fresh_gu[0],
        fresh_down[0],
        server_gu[0],
        server_down[0],
        attn_gain.reshape(1, 2048),
        moe_gain.reshape(1, 2048),
        jnp.cos(angles),
        jnp.sin(angles),
        cache_pos,
        cache_kv[0],
        routes.T,
        router.T,
    )


def solution(mesh):
    placed = (
        P("seq", "tp"),
        P("seq"),
        P("seq", None, None, "tp"),
        P("seq", None),
        P(),
        P(),
        P("seq", None, "tp"),
        P("seq", "tp"),
        P(),
        P("seq", None),
        P(),
        P("seq", "tp", None, None),
        P("seq", "tp", None),
        P("seq", "tp", None, None),
        P("seq", "tp", None),
    )
    return jax.shard_map(
        body, mesh=mesh, in_specs=placed, out_specs=P("seq", "tp"), check_vma=False
    )
```

```python
import functools

import jax
import jax.numpy as jnp
from jax import lax
from jax.experimental import pallas as pl
from jax.experimental.pallas import tpu as pltpu
from jax.sharding import PartitionSpec as P

HEAD_DIM = 128
SINK = 4
WIN = 4096
MESH = pl.DeviceIdType.MESH
BF = jnp.bfloat16
F32 = jnp.float32
ANY = pl.BlockSpec(memory_space=pl.ANY)
VMEM = pl.BlockSpec(memory_space=pltpu.VMEM)
SMEM = pl.BlockSpec(memory_space=pltpu.SMEM)
DMA = pltpu.SemaphoreType.DMA


def places():
    return lax.axis_index("seq"), lax.axis_index("tp")


def greet(peers):
    barrier = pltpu.get_barrier_semaphore()
    for peer in peers:
        pl.semaphore_signal(barrier, inc=1, device_id=peer, device_id_type=MESH)
    pl.semaphore_wait(barrier, len(peers))


def remote(src, dst, send, recv, peer):
    return pltpu.make_async_remote_copy(
        src_ref=src, dst_ref=dst, send_sem=send, recv_sem=recv, device_id=peer, device_id_type=MESH
    )


def push(src, dst, send, recv, peer):
    copy = remote(src, dst, send, recv, peer)
    copy.start()
    return copy


def tp_peers(s, t):
    return [(s, t ^ k) for k in range(1, 8)]


def seq_peer(s, t, k, j):
    z, r = s // 4, s % 4
    return ((z + k) % 8) * 4 + (r ^ j), t


def split_matrix(n):
    row = lax.broadcasted_iota(jnp.int32, (n, n), 0)
    col = lax.broadcasted_iota(jnp.int32, (n, n), 1)
    half = n // 2
    return jnp.where(col == jnp.where(row < half, 2 * row, 2 * (row - half) + 1), 1.0, 0.0).astype(BF)


def nt(a, b):
    return lax.dot_general(a, b, (((1,), (1,)), ((), ())), preferred_element_type=F32)


def slot_rows(rank, first):
    shelf = lax.broadcasted_iota(jnp.int32, (32, 256), 0).astype(F32)
    return [jnp.where(rank[first + e : first + e + 1, :] == shelf, 1.0, 0.0) for e in range(8)]


CHUNKS, WIDTH = 8, 512


def layer_kernel(
    tok,
    context,
    handed,
    qkv,
    proj,
    f_gu,
    f_down,
    s_gu,
    s_down,
    gain,
    moe_gain,
    cosine,
    sine,
    slots,
    cache,
    routes,
    router,
    out,
    hidden,
    rows,
    stats,
    s_gu_out,
    f_gu_out,
    f_down_out,
    o_gu_out,
    o_down_out,
    rank,
    share,
    final,
    wq,
    wo,
    wq_all,
    wo_all,
    tok_all,
    part,
    got,
    qbuf,
    pbuf,
    fbuf,
    sbuf,
    cbuf,
    scores,
    top,
    total,
    acc,
    xn,
    back,
    stats_all,
    stage,
    xstage,
    x,
    y,
    ybuf,
    halves,
    xbuf,
    sums,
    w_down,
    lsem,
    fsem,
    ssem,
    csem,
    tok_s,
    tok_r,
    swap_s,
    swap_r,
    x_s,
    x_r,
    z_s,
    z_r,
    c_s,
    c_r,
    p_s,
    p_r,
    g_s,
    g_r,
    d_s,
    d_r,
    dx_s,
    dx_r,
    dy_s,
    dy_r,
    ry_s,
    ry_r,
    rx_s,
    rx_r,
    r_s,
    r_r,
):
    s, t = places()
    z, xh, c = s // 4, (s // 2) % 2, s % 2
    up = (((z + 1) % 8) * 4 + xh * 2 + c, t)
    down = (((z + 7) % 8) * 4 + xh * 2 + c, t)
    over = (s ^ 2, t)
    twin = (s ^ 1, t)

    pull_q = pltpu.make_async_copy(qkv, qbuf, lsem.at[0])
    pull_p = pltpu.make_async_copy(proj, pbuf, lsem.at[1])
    pull_d = [
        pltpu.make_async_copy(
            f_down.at[:, pl.ds(i * 512, 512)], scores.at[0, i, pl.ds(0, 176)], lsem.at[10 + i]
        )
        for i in range(4)
    ]
    pull_w = pltpu.make_async_copy(s_down, w_down, lsem.at[6])
    pull_q.start()
    pull_p.start()
    for pull in pull_d:
        pull.start()
    f_pulls, s_pulls = [], []
    for col in range(16):
        span = pl.ds(col * 128, 128)
        f_pulls.append(pltpu.make_async_copy(f_gu.at[:, :, span], fbuf.at[col], fsem.at[col]))
        s_pulls.append(pltpu.make_async_copy(s_gu.at[:, :, span], sbuf.at[col], ssem.at[col]))
    for pull in f_pulls:
        pull.start()

    def fetch(i, h):
        span = pl.ds(pl.multiple_of(i * WIDTH, WIDTH), WIDTH)
        return pltpu.make_async_copy(
            cache.at[span, :, pl.ds(h * 128, 128)], cbuf.at[h, span], csem.at[i, h]
        )

    far = [seq_peer(s, t, k, j) for k in range(8) for j in range(4) if (k, j) != (0, 0)]
    greet(tp_peers(s, t) + far)
    spot = tok_all.at[:, pl.ds(pl.multiple_of(t * 256, 256), 256)]
    toks = [push(tok, spot, tok_s.at[k], tok_r.at[k], (s, t ^ k)) for k in range(1, 8)]
    local_t = pltpu.make_async_copy(tok, spot, lsem.at[3])
    local_t.start()
    pull_q.wait()
    for j in range(3):
        wq[:, j * 256 : j * 256 + 256] = qbuf[j].astype(BF)

    class Ring:
        def __init__(self, own, whole, which):
            self.own, self.whole, self.which = own, whole, which
            self.ups, self.downs, self.twins = {}, {}, []

        def block(self, dz, a):
            return self.whole.at[(z + dz + 8) % 8, xh ^ a, c]

        def pass_on(self, src, dst, step, a, ways):
            for way, chain, peer in ((0, self.ups, up), (1, self.downs, down)):
                if way in ways:
                    at = (self.which, way, step, a)
                    chain[(step, a)] = push(src, dst, z_s.at[at], z_r.at[at], peer)

        def to_twin(self, src, dst, place, a):
            at = (self.which, place, a)
            self.twins.append(push(src, dst, c_s.at[at], c_r.at[at], twin))

        def begin(self):
            home = self.block(0, 0)
            self.across = push(self.own, home, x_s.at[self.which], x_r.at[self.which], over)
            self.pass_on(self.own, home, 0, 0, (0, 1))
            self.to_twin(self.own, home, 0, 0)
            self.local = pltpu.make_async_copy(self.own, home, lsem.at[4 + self.which])
            self.local.start()

        def partner(self):
            self.across.wait_recv()
            theirs = self.block(0, 1)
            self.pass_on(theirs, theirs, 0, 1, (0, 1))
            self.to_twin(theirs, theirs, 0, 1)

        def turn(self, step, a, way):
            chain = (self.ups, self.downs)[way]
            if (step, a) not in chain:
                return
            chain[(step, a)].wait_recv()
            dz = (-1 - step, 1 + step)[way]
            here = self.block(dz, a)
            if step < 2 or (step == 2 and a == way):
                self.pass_on(here, here, step + 1, a, (way,))
            self.to_twin(here, here, dz % 8, a)

        def step(self, step):
            for a in range(2):
                for way in range(2):
                    self.turn(step, a, way)

        def arrive(self):
            for copy in self.twins:
                copy.wait_recv()
            self.local.wait()

        def end(self):
            self.across.wait_send()
            for copy in self.twins + list(self.ups.values()) + list(self.downs.values()):
                copy.wait_send()

    ring_q = Ring(wq.at[:, :], wq_all, 0)
    ring_o = Ring(wo.at[:, :], wo_all, 1)
    ring_q.begin()

    f_flat = fbuf.reshape(16, 352, 128)
    s_flat = sbuf.reshape(16, 704, 128)
    c_flat = [cbuf.at[h].reshape(8192, 128) for h in range(2)]
    keys, vals = y.at[0].reshape(4096, 256), y.at[1].reshape(4096, 256)
    swaps = []

    def swap(src, dst):
        i = len(swaps)
        swaps.append(push(src, dst, swap_s.at[i], swap_r.at[i], (s, t ^ 1)))

    def part_fresh():
        for col in range(16):
            f_pulls[col].wait()
            for kind in range(2):
                f_gu_out[kind, :, col * 128 : col * 128 + 128] = f_flat[
                    col, pl.ds(kind, 176, stride=2), :
                ].astype(BF)
        for kind in range(2):
            swap(f_gu_out.at[kind], o_gu_out.at[kind])
        for i in range(CHUNKS):
            for h in range(2):
                fetch(i, h).start()

    def part_down():
        for i in range(4):
            pull_d[i].wait()
            f_down_out[:, i * 512 : i * 512 + 512] = scores[0, i, 0:176].astype(BF)
        for pull in s_pulls:
            pull.start()
        pull_w.start()
        pull_p.wait()
        wo[...] = pbuf[...].astype(BF)

    def part_cache(i):
        for h in range(2):
            fetch(i, h).wait()
        perm = split_matrix(256)
        for k in range(4):
            start = i * 1024 + k * 256
            both = jnp.concatenate([c_flat[h][start : start + 256, :] for h in range(2)], axis=1)
            split = jnp.dot(perm, both, preferred_element_type=F32).astype(BF)
            spot = i * WIDTH + k * 128
            keys[spot : spot + 128, :] = split[0:128]
            vals[spot : spot + 128, :] = split[128:256]

    def part_server(col):
        for pull in s_pulls[2 * col : 2 + 2 * col]:
            pull.wait()
        for first, count in ((0, 256), (256, 256), (512, 192)):
            half = count // 2
            pair = jnp.concatenate(
                [s_flat[2 * col + i, first : first + count, :] for i in range(2)], axis=1
            )
            split = jnp.dot(split_matrix(count), pair, preferred_element_type=F32).astype(BF)
            for kind in range(2):
                s_gu_out[kind, first // 2 : first // 2 + half, col * 256 : col * 256 + 256] = split[
                    kind * half : kind * half + half
                ]

    def part_norm():
        for copy in toks:
            copy.wait_recv()
        local_t.wait()
        field = tok_all[...].astype(F32)
        inv = lax.rsqrt(jnp.mean(field * field, axis=-1, keepdims=True) + 1e-6)
        xn[...] = (field * inv * gain[...]).astype(BF)

    def part_rank():
        shelf = lax.broadcasted_iota(jnp.int32, (64, 256), 0)
        named = (shelf % 32) * 2 + shelf // 32
        hit = jnp.zeros((64, 256), F32)
        for k in range(6):
            hit += jnp.where(routes[k : k + 1, :] == named, 1.0, 0.0)
        row = lax.broadcasted_iota(jnp.int32, (256, 256), 0)
        col = lax.broadcasted_iota(jnp.int32, (256, 256), 1)
        later = jnp.where(row < col, 1.0, 0.0).astype(BF)
        before = jnp.dot(hit.astype(BF), later, preferred_element_type=F32)
        rank[...] = jnp.where(hit > 0.0, before, -1.0)

    work = [functools.partial(part_cache, i) for i in range(8)] + [part_rank]
    work += [functools.partial(part_server, col) for col in range(2)]
    work += [part_norm]
    work += [functools.partial(part_server, col) for col in range(2, 8)]
    part_fresh()
    ring_q.partner()
    part_down()
    for step in range(4):
        for a in range(2):
            for way in range(2):
                ring_q.turn(step, a, way)
                if work:
                    work.pop(0)()
    ring_o.begin()
    for piece in work:
        piece()
    ring_o.partner()
    ring_q.arrive()

    projected = jnp.dot(xn[...], wq_all[...].reshape(2048, 768), preferred_element_type=F32)
    ring_o.step(0)

    cosf = jnp.concatenate([cosine[...], cosine[...]], axis=1)
    sinf = jnp.concatenate([-sine[...], sine[...]], axis=1)

    def turned(field):
        return (field * cosf + pltpu.roll(field, 64, 1) * sinf).astype(BF)

    queries = [turned(projected[:, h * 128 : h * 128 + 128]) for h in range(2)]
    keys_new = [turned(projected[:, 256 + h * 128 : 384 + h * 128]) for h in range(2)]
    values_new = [projected[:, 512 + h * 128 : 640 + h * 128].astype(BF) for h in range(2)]
    row_id = lax.broadcasted_iota(jnp.int32, (256, WIDTH), 0)
    new_row = lax.broadcasted_iota(jnp.int32, (256, 256), 0)
    new_col = lax.broadcasted_iota(jnp.int32, (256, 256), 1)
    for h in range(2):
        fresh = jnp.where(new_col <= new_row, nt(queries[h], keys_new[h]), -1e30)
        scores[h, CHUNKS, :, 0:256] = fresh
        top[h] = jnp.maximum(fresh[:, 0:128], fresh[:, 128:256])

    def score(first, last):
        @pl.loop(first, last)
        def _(i):
            span = pl.ds(pl.multiple_of(i * WIDTH, WIDTH), WIDTH)
            slot = slots[:, span]
            limit = jnp.where(slot < 0, 0, jnp.where(slot < SINK, 256, slot + WIN - context[0]))
            seen = row_id < limit
            for h in range(2):
                block = nt(queries[h], keys[span, h * 128 : h * 128 + 128])
                block = jnp.where(seen, block, -1e30)
                scores[h, i] = block
                peak = jnp.maximum(
                    jnp.maximum(block[:, 0:128], block[:, 128:256]),
                    jnp.maximum(block[:, 256:384], block[:, 384:512]),
                )
                top[h] = jnp.maximum(top[h], peak)

    score(0, 4)
    ring_o.step(1)
    score(4, 8)
    ring_o.step(2)

    scale = 1.4426950408889634 / (HEAD_DIM**0.5)
    for h in range(2):
        top[h] = jnp.broadcast_to(jnp.max(top[h], axis=1, keepdims=True), (256, 128))
        peak = top[h]
        weights = jnp.exp2((scores[h, CHUNKS, :, 0:256] - jnp.tile(peak, (1, 2))) * scale)
        total[h] = weights[:, 0:128] + weights[:, 128:256]
        acc[h] = jnp.dot(weights.astype(BF), values_new[h], preferred_element_type=F32)

    def weigh(first, last):
        @pl.loop(first, last)
        def _(i):
            for h in range(2):
                weights = jnp.exp2((scores[h, i] - jnp.tile(top[h], (1, 4))) * scale)
                total[h] += (weights[:, 0:128] + weights[:, 128:256]) + (
                    weights[:, 256:384] + weights[:, 384:512]
                )
                span = pl.ds(pl.multiple_of(i * WIDTH, WIDTH), WIDTH)
                acc[h] += jnp.dot(
                    weights.astype(BF), vals[span, h * 128 : h * 128 + 128], preferred_element_type=F32
                )

    weigh(0, 4)
    ring_o.step(3)
    weigh(4, 8)
    ring_o.arrive()
    mixed = jnp.concatenate(
        [(acc[h] / jnp.sum(total[h], axis=1, keepdims=True)).astype(BF) for h in range(2)], axis=1
    )

    gives = []
    for k in (2, 6, 1, 3, 4, 5, 7, 0):
        part[k] = nt(mixed, wo_all[t ^ k].reshape(256, 256)).astype(BF)
        if k:
            gives.append(push(part.at[k], got.at[k], p_s.at[k], p_r.at[k], (s, t ^ k)))
    swap(f_down_out, o_down_out)
    for copy in gives:
        copy.wait_recv()
    total_out = tok[...].astype(F32) + part[0].astype(F32)
    for k in range(1, 8):
        total_out += got[k].astype(F32)
    state = total_out.astype(BF)
    hidden[...] = state
    for chunk in range(8):
        pick = jnp.concatenate(slot_rows(rank, chunk * 8), axis=0).astype(BF)
        picked = jnp.dot(pick, state, preferred_element_type=F32).astype(BF)
        first = (chunk % 4) * 8
        rows[chunk // 4, first : first + 8] = picked.reshape(8, 32, 256)
    side, mine = t // 4, t % 2
    cross = (s, t ^ 4)
    r = s % 4
    def distance(i):
        return jnp.where(i == 7, 0, jnp.where(i % 2 == 0, i // 2 + 1, 7 - i // 2))

    def plain(i):
        return (i != 2) & (i != 5)

    def arriving(i, j):
        source = ((z + 8 - distance(i)) % 8) * 4 + (r ^ j)
        return remote(rows.at[:, source], stage.at[:, source], d_s.at[i, j], d_r.at[i, j], (s, t ^ 1))

    def leaving(i, j):
        target = ((z + distance(i)) % 8) * 4 + (r ^ j)
        return remote(rows.at[:, target], stage.at[:, s], d_s.at[i, j], d_r.at[i, j], (target, t))

    def group(i):
        return pl.ds(((z + 8 - distance(i)) % 8) * 4, 4)

    def crossing(i):
        here = group(i)
        return remote(stage.at[:, here], xstage.at[:, here], dx_s.at[i], dx_r.at[i], cross)

    def columns(which):
        owner = t ^ (4 * which)
        return pl.ds(pl.multiple_of(owner * 256, 256), 256)

    def spreading(i, which, m):
        here = group(i)
        buf = (stage, xstage)[which]
        return remote(
            buf.at[(t ^ m) % 2, here],
            x.at[here, :, columns(which)],
            dy_s.at[i, which, m],
            dy_r.at[i, which, m],
            (s, t ^ m),
        )

    def keeping(i, which):
        here = group(i)
        buf = (stage, xstage)[which]
        return pltpu.make_async_copy(
            buf.at[mine, here], x.at[here, :, columns(which)], dy_s.at[i, which, 0]
        )

    def sharing(i, m):
        here = group(i)
        return remote(
            y.at[:, (t ^ m) % 4, here], ybuf.at[m - 1, :, here], ry_s.at[i, m], ry_r.at[i, m], (s, t ^ m)
        )

    def joining(i):
        here = group(i)
        return remote(halves.at[1 - side, :, here], xbuf.at[:, here], rx_s.at[i], rx_r.at[i], cross)

    def returning(i, j):
        target = ((z + 8 - distance(i)) % 8) * 4 + (r ^ j)
        return remote(sums.at[:, target], back.at[:, s], r_s.at[i, j], r_r.at[i, j], (target, t))

    own_in = pltpu.make_async_copy(rows.at[:, s], stage.at[:, s], lsem.at[7])
    own_out = pltpu.make_async_copy(sums.at[:, s], back.at[:, s], lsem.at[8])
    own_in.start()

    @pl.loop(0, 7)
    def _(i):
        for j in range(4):
            leaving(i, j).start()

    for j in range(1, 4):
        leaving(7, j).start()

    def statistics(k):
        return remote(stats, stats_all.at[t], g_s.at[k], g_r.at[k], (s, t ^ k))

    span = pl.ds(pl.multiple_of(t * 256, 256), 256)
    wide = state.astype(F32)
    logits = nt(router[:, span], (wide * moe_gain[:, span]).astype(BF))
    expert = lax.broadcasted_iota(jnp.int32, (64, 256), 0)
    lines = [
        jnp.sum(jnp.where(routes[k : k + 1, :] == expert, logits, 0.0), axis=0, keepdims=True)
        for k in range(6)
    ]
    square = jnp.sum(jnp.transpose(wide * wide), axis=0, keepdims=True)
    stats[...] = jnp.concatenate(lines + [square, jnp.zeros((1, 256), F32)], axis=0)
    near = pltpu.make_async_copy(stats, stats_all.at[t], lsem.at[9])
    near.start()
    for k in range(1, 8):
        statistics(k).start()

    def choose():
        for copy in swaps:
            copy.wait_recv()
        pull_w.wait()
        chosen = jnp.broadcast_to(handed[s], (16, 2048)) == mine
        for first, gu, down in (
            (mine * 176, f_gu_out, f_down_out),
            (176 - mine * 176, o_gu_out, o_down_out),
        ):

            @pl.loop(0, 11)
            def _(i):
                here = pl.ds(pl.multiple_of(i * 16, 16), 16)
                there = pl.ds(pl.multiple_of(first + i * 16, 16), 16)
                for kind in range(2):
                    s_gu_out[kind, there, :] = jnp.where(
                        chosen, gu[kind, here, :].astype(F32), s_gu_out[kind, there, :].astype(F32)
                    ).astype(BF)
                w_down[there, :] = jnp.where(
                    chosen, down[here, :].astype(F32), w_down[there, :].astype(F32)
                ).astype(BF)

    def gates():
        near.wait()
        for k in range(1, 8):
            statistics(k).wait_recv()
        sums_of = stats_all[0]
        for k in range(1, 8):
            sums_of += stats_all[k]
        inv = lax.rsqrt(sums_of[6:7, :] * (1.0 / 2048.0) + 1e-6)
        gate = 1.0 / (1.0 + jnp.exp(-(sums_of * inv)))
        shelf = lax.broadcasted_iota(jnp.int32, (64, 256), 0)
        named = (shelf % 32) * 2 + shelf // 32
        amount = jnp.zeros((64, 256), F32)
        for k in range(6):
            amount += jnp.where(routes[k : k + 1, :] == named, gate[k : k + 1, :], 0.0)
        share[...] = amount
        final[...] = hidden[...].astype(F32)

    def widening(i):
        here = group(i)
        half = x.at[here, :, pl.ds(pl.multiple_of(side * 1024, 1024), 1024)]
        return remote(half, half, dx_s.at[i], dx_r.at[i], cross)

    def arrive(i):
        @pl.when(i == 7)
        def _():
            own_in.wait()

        @pl.when(i < 7)
        def _():
            arriving(i, 0).wait_recv()

        for j in range(1, 4):
            arriving(i, j).wait_recv()

        @pl.when(plain(i))
        def _():
            crossing(i).start()

        for m in range(1, 4):
            spreading(i, 0, m).start()
        keeping(i, 0).start()

    def spread(i):
        @pl.when(plain(i))
        def _():
            crossing(i).wait_recv()
            for m in range(1, 4):
                spreading(i, 1, m).start()
            keeping(i, 1).start()

    def widen(i):
        @pl.when(jnp.logical_not(plain(i)))
        def _():
            for m in range(1, 4):
                spreading(i, 0, m).wait_recv()
            keeping(i, 0).wait()
            widening(i).start()

    def compute(i):
        @pl.when(plain(i))
        def _():
            for which in range(2):
                for m in range(1, 4):
                    spreading(i, which, m).wait_recv()
                keeping(i, which).wait()

        @pl.when(jnp.logical_not(plain(i)))
        def _():
            widening(i).wait_recv()

        here = group(i)
        field = x[here].reshape(128, 2048).astype(F32)
        inv = lax.rsqrt(jnp.mean(field * field, axis=-1, keepdims=True) + 1e-6)
        block = (field * inv * moe_gain[...]).astype(BF)
        gate = nt(block, s_gu_out[0])
        lift = nt(block, s_gu_out[1])
        act = (gate / (1.0 + jnp.exp(-gate)) * lift).astype(BF)
        for part in range(8):
            result = jnp.dot(
                act, w_down[:, part * 256 : part * 256 + 256], preferred_element_type=F32
            )
            y[part // 4, part % 4, here] = result.astype(BF).reshape(4, 32, 256)

        @pl.when(plain(i))
        def _():
            for m in range(1, 4):
                sharing(i, m).start()

        @pl.when(jnp.logical_not(plain(i)))
        def _():
            for pair in range(2):
                leaning(i, pair).start()

    def leaning(i, pair):
        here = group(i)
        send, recv = ((ry_s.at[i, 0], ry_r.at[i, 0]), (rx_s.at[i], rx_r.at[i]))[pair]
        return remote(
            y.at[1 - side, pl.ds(2 * pair, 2), here], ybuf.at[pair, :, here], send, recv, cross
        )

    def landing(i, m):
        here = group(i)
        return (ybuf.at[2, 0, here], ybuf.at[2, 1, here], xbuf.at[0, here])[m - 1]

    def scattering(i, m):
        here = group(i)
        row = (t ^ m) % 4
        return remote(
            halves.at[row // 2, row % 2, here], landing(i, m), ry_s.at[i, m], ry_r.at[i, m], (s, t ^ m)
        )

    def lean(i):
        @pl.when(jnp.logical_not(plain(i)))
        def _():
            here = group(i)
            for pair in range(2):
                leaning(i, pair).wait_recv()
            for row in range(4):
                both = y[side, row, here].astype(F32) + ybuf[row // 2, row % 2, here].astype(F32)
                halves[row // 2, row % 2, here] = both.astype(BF)
            for m in range(1, 4):
                scattering(i, m).start()

    def fold(i):
        @pl.when(plain(i))
        def _():
            fold_plain(i)

    def fold_plain(i):
        here = group(i)
        for m in range(1, 4):
            sharing(i, m).wait_recv()
        for col in range(2):
            same = y[col, t % 4, here].astype(F32) + ybuf[1, col, here].astype(F32)
            halves[col, mine, here] = same.astype(BF)
            other = ybuf[0, col, here].astype(F32) + ybuf[2, col, here].astype(F32)
            halves[col, 1 - mine, here] = other.astype(BF)
        joining(i).start()

    def finish(i):
        here = group(i)

        @pl.when(plain(i))
        def _():
            joining(i).wait_recv()
            for par in range(2):
                both = halves[side, par, here].astype(F32) + xbuf[par, here].astype(F32)
                sums[par, here] = both.astype(BF)

        @pl.when(jnp.logical_not(plain(i)))
        def _():
            for m in range(1, 4):
                scattering(i, m).wait_recv()
            row = t % 4
            same = halves[row // 2, row % 2, here].astype(F32) + ybuf[2, 1, here].astype(F32)
            sums[mine, here] = same.astype(BF)
            other = ybuf[2, 0, here].astype(F32) + xbuf[0, here].astype(F32)
            sums[1 - mine, here] = other.astype(BF)

        @pl.when(i == 7)
        def _():
            own_out.start()

        @pl.when(i < 7)
        def _():
            returning(i, 0).start()

        for j in range(1, 4):
            returning(i, j).start()

    def collect(i):
        @pl.when(i == 7)
        def _():
            own_out.wait()

        @pl.when(i < 7)
        def _():
            returning(i, 0).wait_recv()

        for j in range(1, 4):
            returning(i, j).wait_recv()
        first = ((z + distance(i)) % 8) * 4
        shelf = lax.broadcasted_iota(jnp.int32, (32, 256), 0).astype(F32)
        for par in range(2):
            lines = []
            for e in range(4):
                line = pl.ds(par * 32 + first + e, 1)
                lines.append(jnp.where(rank[line, :] == shelf, share[line, :], 0.0))
            mix = jnp.concatenate(lines, axis=0)
            high = mix.astype(BF)
            low = (mix - high.astype(F32)).astype(BF)
            block = back[par, pl.ds(first, 4)].reshape(128, 256)
            dims = (((0,), (0,)), ((), ()))
            final[...] += lax.dot_general(
                high, block, dims, preferred_element_type=F32
            ) + lax.dot_general(low, block, dims, preferred_element_type=F32)

    @pl.loop(0, 18)
    def _(i):
        @pl.when(i == 3)
        def _():
            choose()

        @pl.when(i == 6)
        def _():
            gates()

        for lag, stage_of in (
            (0, arrive),
            (1, spread),
            (2, widen),
            (3, compute),
            (5, lean),
            (5, fold),
            (7, finish),
            (10, collect),
        ):

            @pl.when((i >= lag) & (i < lag + 8))
            def _():
                stage_of(i - lag)

    out[...] = final[...].astype(BF)
    for k in range(1, 8):
        statistics(k).wait_send()
    for copy in swaps + gives + toks:
        copy.wait_send()
    ring_q.end()
    ring_o.end()

    def settle(i, j):
        leaving(i, j).wait_send()
        returning(i, j).wait_send()

    for j in range(1, 4):
        settle(7, j)

    @pl.loop(0, 7)
    def _(i):
        for j in range(4):
            settle(i, j)

    @pl.loop(0, 8)
    def _(i):
        for m in range(1, 4):
            spreading(i, 0, m).wait_send()

        @pl.when(plain(i))
        def _():
            crossing(i).wait_send()
            joining(i).wait_send()
            for m in range(1, 4):
                sharing(i, m).wait_send()
                spreading(i, 1, m).wait_send()

        @pl.when(jnp.logical_not(plain(i)))
        def _():
            widening(i).wait_send()
            for pair in range(2):
                leaning(i, pair).wait_send()
            for m in range(1, 4):
                scattering(i, m).wait_send()


def layer(*operands):
    return pl.pallas_call(
        layer_kernel,
        out_shape=jax.ShapeDtypeStruct((256, 256), BF),
        in_specs=[VMEM, SMEM, SMEM] + [ANY] * 6 + [VMEM] * 5 + [ANY] + [VMEM] * 2,
        out_specs=VMEM,
        scratch_shapes=[
            pltpu.VMEM((256, 256), BF),
            pltpu.VMEM((2, 32, 32, 256), BF),
            pltpu.VMEM((8, 256), F32),
            pltpu.VMEM((2, 352, 2048), BF),
            pltpu.VMEM((2, 176, 2048), BF),
            pltpu.VMEM((176, 2048), BF),
            pltpu.VMEM((2, 176, 2048), BF),
            pltpu.VMEM((176, 2048), BF),
            pltpu.VMEM((64, 256), F32),
            pltpu.VMEM((64, 256), F32),
            pltpu.VMEM((256, 256), F32),
            pltpu.VMEM((64, 768), BF),
            pltpu.VMEM((64, 256), BF),
            pltpu.VMEM((8, 2, 2, 64, 768), BF),
            pltpu.VMEM((8, 2, 2, 64, 256), BF),
            pltpu.VMEM((256, 2048), BF),
            pltpu.VMEM((8, 256, 256), BF),
            pltpu.VMEM((8, 256, 256), BF),
            pltpu.VMEM((3, 64, 256), F32),
            pltpu.VMEM((64, 256), F32),
            pltpu.VMEM((16, 176, 2, 128), F32),
            pltpu.VMEM((16, 352, 2, 128), BF),
            pltpu.VMEM((2, 4096, 2, 128), BF),
            pltpu.VMEM((2, 9, 256, 512), F32),
            pltpu.VMEM((2, 256, 128), F32),
            pltpu.VMEM((2, 256, 128), F32),
            pltpu.VMEM((2, 256, 128), F32),
            pltpu.VMEM((256, 2048), BF),
            pltpu.VMEM((2, 32, 32, 256), BF),
            pltpu.VMEM((8, 8, 256), F32),
            pltpu.VMEM((2, 32, 32, 256), BF),
            pltpu.VMEM((2, 32, 32, 256), BF),
            pltpu.VMEM((32, 32, 2048), BF),
            pltpu.VMEM((2, 4, 32, 32, 256), BF),
            pltpu.VMEM((3, 2, 32, 32, 256), BF),
            pltpu.VMEM((2, 2, 32, 32, 256), BF),
            pltpu.VMEM((2, 32, 32, 256), BF),
            pltpu.VMEM((2, 32, 32, 256), BF),
            pltpu.VMEM((352, 2048), BF),
            DMA((14,)),
            DMA((16,)),
            DMA((16,)),
            DMA((8, 2)),
            DMA((8,)),
            DMA((8,)),
            DMA((3,)),
            DMA((3,)),
            DMA((2,)),
            DMA((2,)),
            DMA((2, 2, 4, 2)),
            DMA((2, 2, 4, 2)),
            DMA((2, 8, 2)),
            DMA((2, 8, 2)),
            DMA((8,)),
            DMA((8,)),
            DMA((8,)),
            DMA((8,)),
            DMA((8, 4)),
            DMA((8, 4)),
            DMA((8,)),
            DMA((8,)),
            DMA((8, 2, 4)),
            DMA((8, 2, 4)),
            DMA((8, 4)),
            DMA((8, 4)),
            DMA((8,)),
            DMA((8,)),
            DMA((8, 4)),
            DMA((8, 4)),
        ],
        compiler_params=pltpu.CompilerParams(
            collective_id=0, has_side_effects=True, vmem_limit_bytes=60 << 20
        ),
        name="layer",
    )(*operands)


def body(
    tokens,
    ctx_len,
    cache_kv,
    cache_pos,
    attn_gain,
    moe_gain,
    qkv_train,
    out_train,
    router,
    routes,
    handed_half,
    fresh_gu,
    fresh_down,
    server_gu,
    server_down,
):
    half = HEAD_DIM // 2
    frequency = 10000.0 ** (-jnp.arange(half, dtype=F32) / half)
    positions = ctx_len[0] + jnp.arange(256, dtype=jnp.int32)
    angles = positions.astype(F32)[:, None] * frequency[None, :]
    return layer(
        tokens,
        ctx_len,
        handed_half,
        qkv_train.transpose(1, 0, 2),
        out_train,
        fresh_gu[0],
        fresh_down[0],
        server_gu[0],
        server_down[0],
        attn_gain.reshape(1, 2048),
        moe_gain.reshape(1, 2048),
        jnp.cos(angles),
        jnp.sin(angles),
        cache_pos,
        cache_kv[0],
        routes.T,
        router.T,
    )


def solution(mesh):
    placed = (
        P("seq", "tp"),
        P("seq"),
        P("seq", None, None, "tp"),
        P("seq", None),
        P(),
        P(),
        P("seq", None, "tp"),
        P("seq", "tp"),
        P(),
        P("seq", None),
        P(),
        P("seq", "tp", None, None),
        P("seq", "tp", None),
        P("seq", "tp", None, None),
        P("seq", "tp", None),
    )
    return jax.shard_map(
        body, mesh=mesh, in_specs=placed, out_specs=P("seq", "tp"), check_vma=False
    )
```

```python
import functools

import jax
import jax.numpy as jnp
from jax import lax
from jax.experimental import pallas as pl
from jax.experimental.pallas import tpu as pltpu
from jax.sharding import PartitionSpec as P

HEAD_DIM = 128
SINK = 4
WIN = 4096
MESH = pl.DeviceIdType.MESH
BF = jnp.bfloat16
F32 = jnp.float32
ANY = pl.BlockSpec(memory_space=pl.ANY)
VMEM = pl.BlockSpec(memory_space=pltpu.VMEM)
SMEM = pl.BlockSpec(memory_space=pltpu.SMEM)
DMA = pltpu.SemaphoreType.DMA


def places():
    return lax.axis_index("seq"), lax.axis_index("tp")


def greet(peers):
    barrier = pltpu.get_barrier_semaphore()
    for peer in peers:
        pl.semaphore_signal(barrier, inc=1, device_id=peer, device_id_type=MESH)
    pl.semaphore_wait(barrier, len(peers))


def remote(src, dst, send, recv, peer):
    return pltpu.make_async_remote_copy(
        src_ref=src, dst_ref=dst, send_sem=send, recv_sem=recv, device_id=peer, device_id_type=MESH
    )


def push(src, dst, send, recv, peer):
    copy = remote(src, dst, send, recv, peer)
    copy.start()
    return copy


def tp_peers(s, t):
    return [(s, t ^ k) for k in range(1, 8)]


def seq_peer(s, t, k, j):
    z, r = s // 4, s % 4
    return ((z + k) % 8) * 4 + (r ^ j), t


def split_matrix(n):
    row = lax.broadcasted_iota(jnp.int32, (n, n), 0)
    col = lax.broadcasted_iota(jnp.int32, (n, n), 1)
    half = n // 2
    return jnp.where(col == jnp.where(row < half, 2 * row, 2 * (row - half) + 1), 1.0, 0.0).astype(BF)


def nt(a, b):
    return lax.dot_general(a, b, (((1,), (1,)), ((), ())), preferred_element_type=F32)


def slot_rows(rank, first):
    shelf = lax.broadcasted_iota(jnp.int32, (32, 256), 0).astype(F32)
    return [jnp.where(rank[first + e : first + e + 1, :] == shelf, 1.0, 0.0) for e in range(8)]


CHUNKS, WIDTH = 8, 512
TOKEN_ORDER = (4, 6, 2, 5, 7, 1, 3)


def layer_kernel(
    tok,
    context,
    handed,
    qkv,
    proj,
    f_gu,
    f_down,
    s_gu,
    s_down,
    gain,
    moe_gain,
    cosine,
    sine,
    slots,
    cache,
    routes,
    router,
    out,
    hidden,
    rows,
    stats,
    s_gu_out,
    f_gu_out,
    f_down_out,
    o_gu_out,
    o_down_out,
    rank,
    share,
    final,
    wq,
    wo,
    wq_all,
    wo_all,
    tok_all,
    part,
    got,
    qbuf,
    pbuf,
    fbuf,
    sbuf,
    cbuf,
    scores,
    top,
    total,
    acc,
    xn,
    back,
    stats_all,
    stage,
    xstage,
    x,
    y,
    ybuf,
    halves,
    xbuf,
    sums,
    w_down,
    lsem,
    fsem,
    ssem,
    csem,
    tok_s,
    tok_r,
    swap_s,
    swap_r,
    x_s,
    x_r,
    z_s,
    z_r,
    c_s,
    c_r,
    p_s,
    p_r,
    g_s,
    g_r,
    d_s,
    d_r,
    dx_s,
    dx_r,
    dy_s,
    dy_r,
    ry_s,
    ry_r,
    rx_s,
    rx_r,
    r_s,
    r_r,
):
    s, t = places()
    z, xh, c = s // 4, (s // 2) % 2, s % 2
    up = (((z + 1) % 8) * 4 + xh * 2 + c, t)
    down = (((z + 7) % 8) * 4 + xh * 2 + c, t)
    over = (s ^ 2, t)
    twin = (s ^ 1, t)

    pull_q = pltpu.make_async_copy(qkv, qbuf, lsem.at[0])
    pull_p = pltpu.make_async_copy(proj, pbuf, lsem.at[1])
    pull_d = [
        pltpu.make_async_copy(
            f_down.at[:, pl.ds(i * 512, 512)], scores.at[0, i, pl.ds(0, 176)], lsem.at[10 + i]
        )
        for i in range(4)
    ]
    pull_w = pltpu.make_async_copy(s_down, w_down, lsem.at[6])
    pull_q.start()
    pull_p.start()
    for pull in pull_d:
        pull.start()
    f_pulls, s_pulls = [], []
    for col in range(16):
        span = pl.ds(col * 128, 128)
        f_pulls.append(pltpu.make_async_copy(f_gu.at[:, :, span], fbuf.at[col], fsem.at[col]))
        s_pulls.append(pltpu.make_async_copy(s_gu.at[:, :, span], sbuf.at[col], ssem.at[col]))
    for pull in f_pulls:
        pull.start()

    def fetch(i, h):
        span = pl.ds(pl.multiple_of(i * WIDTH, WIDTH), WIDTH)
        return pltpu.make_async_copy(
            cache.at[span, :, pl.ds(h * 128, 128)], cbuf.at[h, span], csem.at[i, h]
        )

    far = [seq_peer(s, t, k, j) for k in range(8) for j in range(4) if (k, j) != (0, 0)]
    greet(tp_peers(s, t) + far)
    spot = tok_all.at[:, pl.ds(pl.multiple_of(t * 256, 256), 256)]
    toks = []

    def share_tokens(count):
        for k in TOKEN_ORDER[len(toks) : len(toks) + count]:
            toks.append(push(tok, spot, tok_s.at[k], tok_r.at[k], (s, t ^ k)))

    local_t = pltpu.make_async_copy(tok, spot, lsem.at[3])
    local_t.start()
    pull_q.wait()
    for j in range(3):
        wq[:, j * 256 : j * 256 + 256] = qbuf[j].astype(BF)

    class Ring:
        def __init__(self, own, whole, which):
            self.own, self.whole, self.which = own, whole, which
            self.ups, self.downs, self.twins = {}, {}, []

        def block(self, dz, a):
            return self.whole.at[(z + dz + 8) % 8, xh ^ a, c]

        def pass_on(self, src, dst, step, a, ways):
            for way, chain, peer in ((0, self.ups, up), (1, self.downs, down)):
                if way in ways:
                    at = (self.which, way, step, a)
                    chain[(step, a)] = push(src, dst, z_s.at[at], z_r.at[at], peer)

        def to_twin(self, src, dst, place, a):
            at = (self.which, place, a)
            self.twins.append(push(src, dst, c_s.at[at], c_r.at[at], twin))

        def begin(self):
            home = self.block(0, 0)
            self.across = push(self.own, home, x_s.at[self.which], x_r.at[self.which], over)
            self.pass_on(self.own, home, 0, 0, (0, 1))
            self.to_twin(self.own, home, 0, 0)
            self.local = pltpu.make_async_copy(self.own, home, lsem.at[4 + self.which])
            self.local.start()

        def partner(self):
            self.across.wait_recv()
            theirs = self.block(0, 1)
            self.pass_on(theirs, theirs, 0, 1, (0, 1))
            self.to_twin(theirs, theirs, 0, 1)

        def turn(self, step, a, way):
            chain = (self.ups, self.downs)[way]
            if (step, a) not in chain:
                return
            chain[(step, a)].wait_recv()
            dz = (-1 - step, 1 + step)[way]
            here = self.block(dz, a)
            if step < 2 or (step == 2 and a == way):
                self.pass_on(here, here, step + 1, a, (way,))
            self.to_twin(here, here, dz % 8, a)

        def step(self, step):
            for a in range(2):
                for way in range(2):
                    self.turn(step, a, way)

        def arrive(self):
            for copy in self.twins:
                copy.wait_recv()
            self.local.wait()

        def end(self):
            self.across.wait_send()
            for copy in self.twins + list(self.ups.values()) + list(self.downs.values()):
                copy.wait_send()

    ring_q = Ring(wq.at[:, :], wq_all, 0)
    ring_o = Ring(wo.at[:, :], wo_all, 1)
    ring_q.begin()

    f_flat = fbuf.reshape(16, 352, 128)
    s_flat = sbuf.reshape(16, 704, 128)
    c_flat = [cbuf.at[h].reshape(8192, 128) for h in range(2)]
    keys, vals = y.at[0].reshape(4096, 256), y.at[1].reshape(4096, 256)
    swaps = []

    def swap(src, dst):
        i = len(swaps)
        swaps.append(push(src, dst, swap_s.at[i], swap_r.at[i], (s, t ^ 1)))

    def part_fresh():
        for col in range(16):
            f_pulls[col].wait()
            for kind in range(2):
                f_gu_out[kind, :, col * 128 : col * 128 + 128] = f_flat[
                    col, pl.ds(kind, 176, stride=2), :
                ].astype(BF)
        for i in range(CHUNKS):
            for h in range(2):
                fetch(i, h).start()

    def part_down():
        for i in range(4):
            pull_d[i].wait()
            f_down_out[:, i * 512 : i * 512 + 512] = scores[0, i, 0:176].astype(BF)
        for pull in s_pulls:
            pull.start()
        pull_w.start()
        pull_p.wait()
        wo[...] = pbuf[...].astype(BF)

    def part_cache(i):
        for h in range(2):
            fetch(i, h).wait()
        perm = split_matrix(256)
        for k in range(4):
            start = i * 1024 + k * 256
            both = jnp.concatenate([c_flat[h][start : start + 256, :] for h in range(2)], axis=1)
            split = jnp.dot(perm, both, preferred_element_type=F32).astype(BF)
            spot = i * WIDTH + k * 128
            keys[spot : spot + 128, :] = split[0:128]
            vals[spot : spot + 128, :] = split[128:256]

    def part_server(col):
        for pull in s_pulls[2 * col : 2 + 2 * col]:
            pull.wait()
        for first, count in ((0, 256), (256, 256), (512, 192)):
            half = count // 2
            pair = jnp.concatenate(
                [s_flat[2 * col + i, first : first + count, :] for i in range(2)], axis=1
            )
            split = jnp.dot(split_matrix(count), pair, preferred_element_type=F32).astype(BF)
            for kind in range(2):
                s_gu_out[kind, first // 2 : first // 2 + half, col * 256 : col * 256 + 256] = split[
                    kind * half : kind * half + half
                ]

    def part_norm():
        for copy in toks:
            copy.wait_recv()
        local_t.wait()
        field = tok_all[...].astype(F32)
        inv = lax.rsqrt(jnp.mean(field * field, axis=-1, keepdims=True) + 1e-6)
        xn[...] = (field * inv * gain[...]).astype(BF)

    def part_rank():
        shelf = lax.broadcasted_iota(jnp.int32, (64, 256), 0)
        named = (shelf % 32) * 2 + shelf // 32
        hit = jnp.zeros((64, 256), F32)
        for k in range(6):
            hit += jnp.where(routes[k : k + 1, :] == named, 1.0, 0.0)
        row = lax.broadcasted_iota(jnp.int32, (256, 256), 0)
        col = lax.broadcasted_iota(jnp.int32, (256, 256), 1)
        later = jnp.where(row < col, 1.0, 0.0).astype(BF)
        before = jnp.dot(hit.astype(BF), later, preferred_element_type=F32)
        rank[...] = jnp.where(hit > 0.0, before, -1.0)

    work = [functools.partial(part_cache, i) for i in range(8)] + [part_rank]
    work += [functools.partial(part_server, col) for col in range(2)]
    work += [part_norm]
    work += [functools.partial(part_server, col) for col in range(2, 8)]
    ring_q.partner()
    part_fresh()
    part_down()
    event = 0
    for step in range(4):
        for a in range(2):
            for way in range(2):
                if (step, a) not in (ring_q.ups, ring_q.downs)[way]:
                    continue
                ring_q.turn(step, a, way)
                share_tokens(1)
                if event in (7, 8):
                    swap(f_gu_out.at[event - 7], o_gu_out.at[event - 7])
                if event == 4:
                    ring_o.begin()
                if event == 7:
                    ring_o.partner()
                if event == 9:
                    ring_o.step(0)
                if event == 12:
                    ring_o.step(1)
                event += 1
                if work:
                    work.pop(0)()
    for piece in work:
        piece()
    ring_q.arrive()

    projected = jnp.dot(xn[...], wq_all[...].reshape(2048, 768), preferred_element_type=F32)

    cosf = jnp.concatenate([cosine[...], cosine[...]], axis=1)
    sinf = jnp.concatenate([-sine[...], sine[...]], axis=1)

    def turned(field):
        return (field * cosf + pltpu.roll(field, 64, 1) * sinf).astype(BF)

    queries = [turned(projected[:, h * 128 : h * 128 + 128]) for h in range(2)]
    keys_new = [turned(projected[:, 256 + h * 128 : 384 + h * 128]) for h in range(2)]
    values_new = [projected[:, 512 + h * 128 : 640 + h * 128].astype(BF) for h in range(2)]
    row_id = lax.broadcasted_iota(jnp.int32, (256, WIDTH), 0)
    new_row = lax.broadcasted_iota(jnp.int32, (256, 256), 0)
    new_col = lax.broadcasted_iota(jnp.int32, (256, 256), 1)
    for h in range(2):
        fresh = jnp.where(new_col <= new_row, nt(queries[h], keys_new[h]), -1e30)
        scores[h, CHUNKS, :, 0:256] = fresh
        top[h] = jnp.maximum(fresh[:, 0:128], fresh[:, 128:256])

    def score(first, last):
        @pl.loop(first, last)
        def _(i):
            span = pl.ds(pl.multiple_of(i * WIDTH, WIDTH), WIDTH)
            slot = slots[:, span]
            limit = jnp.where(slot < 0, 0, jnp.where(slot < SINK, 256, slot + WIN - context[0]))
            seen = row_id < limit
            for h in range(2):
                block = nt(queries[h], keys[span, h * 128 : h * 128 + 128])
                block = jnp.where(seen, block, -1e30)
                scores[h, i] = block
                peak = jnp.maximum(
                    jnp.maximum(block[:, 0:128], block[:, 128:256]),
                    jnp.maximum(block[:, 256:384], block[:, 384:512]),
                )
                top[h] = jnp.maximum(top[h], peak)

    score(0, 4)
    ring_o.step(2)
    score(4, 8)

    scale = 1.4426950408889634 / (HEAD_DIM**0.5)
    for h in range(2):
        top[h] = jnp.broadcast_to(jnp.max(top[h], axis=1, keepdims=True), (256, 128))
        peak = top[h]
        weights = jnp.exp2((scores[h, CHUNKS, :, 0:256] - jnp.tile(peak, (1, 2))) * scale)
        total[h] = weights[:, 0:128] + weights[:, 128:256]
        acc[h] = jnp.dot(weights.astype(BF), values_new[h], preferred_element_type=F32)

    def weigh(first, last):
        @pl.loop(first, last)
        def _(i):
            for h in range(2):
                weights = jnp.exp2((scores[h, i] - jnp.tile(top[h], (1, 4))) * scale)
                total[h] += (weights[:, 0:128] + weights[:, 128:256]) + (
                    weights[:, 256:384] + weights[:, 384:512]
                )
                span = pl.ds(pl.multiple_of(i * WIDTH, WIDTH), WIDTH)
                acc[h] += jnp.dot(
                    weights.astype(BF), vals[span, h * 128 : h * 128 + 128], preferred_element_type=F32
                )

    ring_o.step(3)
    weigh(0, 8)
    ring_o.arrive()
    mixed = jnp.concatenate(
        [(acc[h] / jnp.sum(total[h], axis=1, keepdims=True)).astype(BF) for h in range(2)], axis=1
    )

    gives = []
    for k in (2, 6, 1, 3, 4, 5, 7, 0):
        part[k] = nt(mixed, wo_all[t ^ k].reshape(256, 256)).astype(BF)
        if k:
            gives.append(push(part.at[k], got.at[k], p_s.at[k], p_r.at[k], (s, t ^ k)))
    swap(f_down_out, o_down_out)
    for copy in gives:
        copy.wait_recv()
    total_out = tok[...].astype(F32) + part[0].astype(F32)
    for k in range(1, 8):
        total_out += got[k].astype(F32)
    state = total_out.astype(BF)
    hidden[...] = state
    for chunk in range(8):
        pick = jnp.concatenate(slot_rows(rank, chunk * 8), axis=0).astype(BF)
        picked = jnp.dot(pick, state, preferred_element_type=F32).astype(BF)
        first = (chunk % 4) * 8
        rows[chunk // 4, first : first + 8] = picked.reshape(8, 32, 256)
    side, mine = t // 4, t % 2
    cross = (s, t ^ 4)
    r = s % 4
    def distance(i):
        return jnp.where(i == 7, 0, jnp.where(i % 2 == 0, i // 2 + 1, 7 - i // 2))

    def plain(i):
        return (i != 2) & (i != 5)

    def arriving(i, j):
        source = ((z + 8 - distance(i)) % 8) * 4 + (r ^ j)
        return remote(rows.at[:, source], stage.at[:, source], d_s.at[i, j], d_r.at[i, j], (s, t ^ 1))

    def leaving(i, j):
        target = ((z + distance(i)) % 8) * 4 + (r ^ j)
        return remote(rows.at[:, target], stage.at[:, s], d_s.at[i, j], d_r.at[i, j], (target, t))

    def group(i):
        return pl.ds(((z + 8 - distance(i)) % 8) * 4, 4)

    def crossing(i):
        here = group(i)
        return remote(stage.at[:, here], xstage.at[:, here], dx_s.at[i], dx_r.at[i], cross)

    def columns(which):
        owner = t ^ (4 * which)
        return pl.ds(pl.multiple_of(owner * 256, 256), 256)

    def spreading(i, which, m):
        here = group(i)
        buf = (stage, xstage)[which]
        return remote(
            buf.at[(t ^ m) % 2, here],
            x.at[here, :, columns(which)],
            dy_s.at[i, which, m],
            dy_r.at[i, which, m],
            (s, t ^ m),
        )

    def keeping(i, which):
        here = group(i)
        buf = (stage, xstage)[which]
        return pltpu.make_async_copy(
            buf.at[mine, here], x.at[here, :, columns(which)], dy_s.at[i, which, 0]
        )

    def sharing(i, m):
        here = group(i)
        return remote(
            y.at[:, (t ^ m) % 4, here], ybuf.at[m - 1, :, here], ry_s.at[i, m], ry_r.at[i, m], (s, t ^ m)
        )

    def joining(i):
        here = group(i)
        return remote(halves.at[1 - side, :, here], xbuf.at[:, here], rx_s.at[i], rx_r.at[i], cross)

    def returning(i, j):
        target = ((z + 8 - distance(i)) % 8) * 4 + (r ^ j)
        return remote(sums.at[:, target], back.at[:, s], r_s.at[i, j], r_r.at[i, j], (target, t))

    own_in = pltpu.make_async_copy(rows.at[:, s], stage.at[:, s], lsem.at[7])
    own_out = pltpu.make_async_copy(sums.at[:, s], back.at[:, s], lsem.at[8])
    own_in.start()

    @pl.loop(0, 7)
    def _(i):
        for j in range(4):
            leaving(i, j).start()

    for j in range(1, 4):
        leaving(7, j).start()

    def statistics(k):
        return remote(stats, stats_all.at[t], g_s.at[k], g_r.at[k], (s, t ^ k))

    span = pl.ds(pl.multiple_of(t * 256, 256), 256)
    wide = state.astype(F32)
    logits = nt(router[:, span], (wide * moe_gain[:, span]).astype(BF))
    expert = lax.broadcasted_iota(jnp.int32, (64, 256), 0)
    lines = [
        jnp.sum(jnp.where(routes[k : k + 1, :] == expert, logits, 0.0), axis=0, keepdims=True)
        for k in range(6)
    ]
    square = jnp.sum(jnp.transpose(wide * wide), axis=0, keepdims=True)
    stats[...] = jnp.concatenate(lines + [square, jnp.zeros((1, 256), F32)], axis=0)
    near = pltpu.make_async_copy(stats, stats_all.at[t], lsem.at[9])
    near.start()
    for k in range(1, 8):
        statistics(k).start()

    def choose():
        for copy in swaps:
            copy.wait_recv()
        pull_w.wait()
        chosen = jnp.broadcast_to(handed[s], (16, 2048)) == mine
        for first, gu, down in (
            (mine * 176, f_gu_out, f_down_out),
            (176 - mine * 176, o_gu_out, o_down_out),
        ):

            @pl.loop(0, 11)
            def _(i):
                here = pl.ds(pl.multiple_of(i * 16, 16), 16)
                there = pl.ds(pl.multiple_of(first + i * 16, 16), 16)
                for kind in range(2):
                    s_gu_out[kind, there, :] = jnp.where(
                        chosen, gu[kind, here, :].astype(F32), s_gu_out[kind, there, :].astype(F32)
                    ).astype(BF)
                w_down[there, :] = jnp.where(
                    chosen, down[here, :].astype(F32), w_down[there, :].astype(F32)
                ).astype(BF)

    def gates():
        near.wait()
        for k in range(1, 8):
            statistics(k).wait_recv()
        sums_of = stats_all[0]
        for k in range(1, 8):
            sums_of += stats_all[k]
        inv = lax.rsqrt(sums_of[6:7, :] * (1.0 / 2048.0) + 1e-6)
        gate = 1.0 / (1.0 + jnp.exp(-(sums_of * inv)))
        shelf = lax.broadcasted_iota(jnp.int32, (64, 256), 0)
        named = (shelf % 32) * 2 + shelf // 32
        amount = jnp.zeros((64, 256), F32)
        for k in range(6):
            amount += jnp.where(routes[k : k + 1, :] == named, gate[k : k + 1, :], 0.0)
        share[...] = amount
        final[...] = hidden[...].astype(F32)

    def widening(i):
        here = group(i)
        half = x.at[here, :, pl.ds(pl.multiple_of(side * 1024, 1024), 1024)]
        return remote(half, half, dx_s.at[i], dx_r.at[i], cross)

    def arrive(i):
        @pl.when(i == 7)
        def _():
            own_in.wait()

        @pl.when(i < 7)
        def _():
            arriving(i, 0).wait_recv()

        for j in range(1, 4):
            arriving(i, j).wait_recv()

        @pl.when(plain(i))
        def _():
            crossing(i).start()

        for m in range(1, 4):
            spreading(i, 0, m).start()
        keeping(i, 0).start()

    def spread(i):
        @pl.when(plain(i))
        def _():
            crossing(i).wait_recv()
            for m in range(1, 4):
                spreading(i, 1, m).start()
            keeping(i, 1).start()

    def widen(i):
        @pl.when(jnp.logical_not(plain(i)))
        def _():
            for m in range(1, 4):
                spreading(i, 0, m).wait_recv()
            keeping(i, 0).wait()
            widening(i).start()

    def compute(i):
        @pl.when(plain(i))
        def _():
            for which in range(2):
                for m in range(1, 4):
                    spreading(i, which, m).wait_recv()
                keeping(i, which).wait()

        @pl.when(jnp.logical_not(plain(i)))
        def _():
            widening(i).wait_recv()

        here = group(i)
        field = x[here].reshape(128, 2048).astype(F32)
        inv = lax.rsqrt(jnp.mean(field * field, axis=-1, keepdims=True) + 1e-6)
        block = (field * inv * moe_gain[...]).astype(BF)
        gate = nt(block, s_gu_out[0])
        lift = nt(block, s_gu_out[1])
        act = (gate / (1.0 + jnp.exp(-gate)) * lift).astype(BF)
        for part in range(8):
            result = jnp.dot(
                act, w_down[:, part * 256 : part * 256 + 256], preferred_element_type=F32
            )
            y[part // 4, part % 4, here] = result.astype(BF).reshape(4, 32, 256)

        @pl.when(plain(i))
        def _():
            for m in range(1, 4):
                sharing(i, m).start()

        @pl.when(jnp.logical_not(plain(i)))
        def _():
            for pair in range(2):
                leaning(i, pair).start()

    def leaning(i, pair):
        here = group(i)
        send, recv = ((ry_s.at[i, 0], ry_r.at[i, 0]), (rx_s.at[i], rx_r.at[i]))[pair]
        return remote(
            y.at[1 - side, pl.ds(2 * pair, 2), here], ybuf.at[pair, :, here], send, recv, cross
        )

    def landing(i, m):
        here = group(i)
        return (ybuf.at[2, 0, here], ybuf.at[2, 1, here], xbuf.at[0, here])[m - 1]

    def scattering(i, m):
        here = group(i)
        row = (t ^ m) % 4
        return remote(
            halves.at[row // 2, row % 2, here], landing(i, m), ry_s.at[i, m], ry_r.at[i, m], (s, t ^ m)
        )

    def lean(i):
        @pl.when(jnp.logical_not(plain(i)))
        def _():
            here = group(i)
            for pair in range(2):
                leaning(i, pair).wait_recv()
            for row in range(4):
                both = y[side, row, here].astype(F32) + ybuf[row // 2, row % 2, here].astype(F32)
                halves[row // 2, row % 2, here] = both.astype(BF)
            for m in range(1, 4):
                scattering(i, m).start()

    def fold(i):
        @pl.when(plain(i))
        def _():
            fold_plain(i)

    def fold_plain(i):
        here = group(i)
        for m in range(1, 4):
            sharing(i, m).wait_recv()
        for col in range(2):
            same = y[col, t % 4, here].astype(F32) + ybuf[1, col, here].astype(F32)
            halves[col, mine, here] = same.astype(BF)
            other = ybuf[0, col, here].astype(F32) + ybuf[2, col, here].astype(F32)
            halves[col, 1 - mine, here] = other.astype(BF)
        joining(i).start()

    def finish(i):
        here = group(i)

        @pl.when(plain(i))
        def _():
            joining(i).wait_recv()
            for par in range(2):
                both = halves[side, par, here].astype(F32) + xbuf[par, here].astype(F32)
                sums[par, here] = both.astype(BF)

        @pl.when(jnp.logical_not(plain(i)))
        def _():
            for m in range(1, 4):
                scattering(i, m).wait_recv()
            row = t % 4
            same = halves[row // 2, row % 2, here].astype(F32) + ybuf[2, 1, here].astype(F32)
            sums[mine, here] = same.astype(BF)
            other = ybuf[2, 0, here].astype(F32) + xbuf[0, here].astype(F32)
            sums[1 - mine, here] = other.astype(BF)

        @pl.when(i == 7)
        def _():
            own_out.start()

        @pl.when(i < 7)
        def _():
            returning(i, 0).start()

        for j in range(1, 4):
            returning(i, j).start()

    def collect(i):
        @pl.when(i == 7)
        def _():
            own_out.wait()

        @pl.when(i < 7)
        def _():
            returning(i, 0).wait_recv()

        for j in range(1, 4):
            returning(i, j).wait_recv()
        first = ((z + distance(i)) % 8) * 4
        shelf = lax.broadcasted_iota(jnp.int32, (32, 256), 0).astype(F32)
        for par in range(2):
            lines = []
            for e in range(4):
                line = pl.ds(par * 32 + first + e, 1)
                lines.append(jnp.where(rank[line, :] == shelf, share[line, :], 0.0))
            mix = jnp.concatenate(lines, axis=0)
            high = mix.astype(BF)
            low = (mix - high.astype(F32)).astype(BF)
            block = back[par, pl.ds(first, 4)].reshape(128, 256)
            dims = (((0,), (0,)), ((), ()))
            final[...] += lax.dot_general(
                high, block, dims, preferred_element_type=F32
            ) + lax.dot_general(low, block, dims, preferred_element_type=F32)

    @pl.loop(0, 18)
    def _(i):
        @pl.when(i == 3)
        def _():
            choose()

        @pl.when(i == 6)
        def _():
            gates()

        for lag, stage_of in (
            (0, arrive),
            (1, spread),
            (2, widen),
            (3, compute),
            (5, lean),
            (5, fold),
            (7, finish),
            (10, collect),
        ):

            @pl.when((i >= lag) & (i < lag + 8))
            def _():
                stage_of(i - lag)

    out[...] = final[...].astype(BF)
    for k in range(1, 8):
        statistics(k).wait_send()
    for copy in swaps + gives + toks:
        copy.wait_send()
    ring_q.end()
    ring_o.end()

    def settle(i, j):
        leaving(i, j).wait_send()
        returning(i, j).wait_send()

    for j in range(1, 4):
        settle(7, j)

    @pl.loop(0, 7)
    def _(i):
        for j in range(4):
            settle(i, j)

    @pl.loop(0, 8)
    def _(i):
        for m in range(1, 4):
            spreading(i, 0, m).wait_send()

        @pl.when(plain(i))
        def _():
            crossing(i).wait_send()
            joining(i).wait_send()
            for m in range(1, 4):
                sharing(i, m).wait_send()
                spreading(i, 1, m).wait_send()

        @pl.when(jnp.logical_not(plain(i)))
        def _():
            widening(i).wait_send()
            for pair in range(2):
                leaning(i, pair).wait_send()
            for m in range(1, 4):
                scattering(i, m).wait_send()


def layer(*operands):
    return pl.pallas_call(
        layer_kernel,
        out_shape=jax.ShapeDtypeStruct((256, 256), BF),
        in_specs=[VMEM, SMEM, SMEM] + [ANY] * 6 + [VMEM] * 5 + [ANY] + [VMEM] * 2,
        out_specs=VMEM,
        scratch_shapes=[
            pltpu.VMEM((256, 256), BF),
            pltpu.VMEM((2, 32, 32, 256), BF),
            pltpu.VMEM((8, 256), F32),
            pltpu.VMEM((2, 352, 2048), BF),
            pltpu.VMEM((2, 176, 2048), BF),
            pltpu.VMEM((176, 2048), BF),
            pltpu.VMEM((2, 176, 2048), BF),
            pltpu.VMEM((176, 2048), BF),
            pltpu.VMEM((64, 256), F32),
            pltpu.VMEM((64, 256), F32),
            pltpu.VMEM((256, 256), F32),
            pltpu.VMEM((64, 768), BF),
            pltpu.VMEM((64, 256), BF),
            pltpu.VMEM((8, 2, 2, 64, 768), BF),
            pltpu.VMEM((8, 2, 2, 64, 256), BF),
            pltpu.VMEM((256, 2048), BF),
            pltpu.VMEM((8, 256, 256), BF),
            pltpu.VMEM((8, 256, 256), BF),
            pltpu.VMEM((3, 64, 256), F32),
            pltpu.VMEM((64, 256), F32),
            pltpu.VMEM((16, 176, 2, 128), F32),
            pltpu.VMEM((16, 352, 2, 128), BF),
            pltpu.VMEM((2, 4096, 2, 128), BF),
            pltpu.VMEM((2, 9, 256, 512), F32),
            pltpu.VMEM((2, 256, 128), F32),
            pltpu.VMEM((2, 256, 128), F32),
            pltpu.VMEM((2, 256, 128), F32),
            pltpu.VMEM((256, 2048), BF),
            pltpu.VMEM((2, 32, 32, 256), BF),
            pltpu.VMEM((8, 8, 256), F32),
            pltpu.VMEM((2, 32, 32, 256), BF),
            pltpu.VMEM((2, 32, 32, 256), BF),
            pltpu.VMEM((32, 32, 2048), BF),
            pltpu.VMEM((2, 4, 32, 32, 256), BF),
            pltpu.VMEM((3, 2, 32, 32, 256), BF),
            pltpu.VMEM((2, 2, 32, 32, 256), BF),
            pltpu.VMEM((2, 32, 32, 256), BF),
            pltpu.VMEM((2, 32, 32, 256), BF),
            pltpu.VMEM((352, 2048), BF),
            DMA((14,)),
            DMA((16,)),
            DMA((16,)),
            DMA((8, 2)),
            DMA((8,)),
            DMA((8,)),
            DMA((3,)),
            DMA((3,)),
            DMA((2,)),
            DMA((2,)),
            DMA((2, 2, 4, 2)),
            DMA((2, 2, 4, 2)),
            DMA((2, 8, 2)),
            DMA((2, 8, 2)),
            DMA((8,)),
            DMA((8,)),
            DMA((8,)),
            DMA((8,)),
            DMA((8, 4)),
            DMA((8, 4)),
            DMA((8,)),
            DMA((8,)),
            DMA((8, 2, 4)),
            DMA((8, 2, 4)),
            DMA((8, 4)),
            DMA((8, 4)),
            DMA((8,)),
            DMA((8,)),
            DMA((8, 4)),
            DMA((8, 4)),
        ],
        compiler_params=pltpu.CompilerParams(
            collective_id=0, has_side_effects=True, vmem_limit_bytes=60 << 20
        ),
        name="layer",
    )(*operands)


def body(
    tokens,
    ctx_len,
    cache_kv,
    cache_pos,
    attn_gain,
    moe_gain,
    qkv_train,
    out_train,
    router,
    routes,
    handed_half,
    fresh_gu,
    fresh_down,
    server_gu,
    server_down,
):
    half = HEAD_DIM // 2
    frequency = 10000.0 ** (-jnp.arange(half, dtype=F32) / half)
    positions = ctx_len[0] + jnp.arange(256, dtype=jnp.int32)
    angles = positions.astype(F32)[:, None] * frequency[None, :]
    return layer(
        tokens,
        ctx_len,
        handed_half,
        qkv_train.transpose(1, 0, 2),
        out_train,
        fresh_gu[0],
        fresh_down[0],
        server_gu[0],
        server_down[0],
        attn_gain.reshape(1, 2048),
        moe_gain.reshape(1, 2048),
        jnp.cos(angles),
        jnp.sin(angles),
        cache_pos,
        cache_kv[0],
        routes.T,
        router.T,
    )


def solution(mesh):
    placed = (
        P("seq", "tp"),
        P("seq"),
        P("seq", None, None, "tp"),
        P("seq", None),
        P(),
        P(),
        P("seq", None, "tp"),
        P("seq", "tp"),
        P(),
        P("seq", None),
        P(),
        P("seq", "tp", None, None),
        P("seq", "tp", None),
        P("seq", "tp", None, None),
        P("seq", "tp", None),
    )
    return jax.shard_map(
        body, mesh=mesh, in_specs=placed, out_specs=P("seq", "tp"), check_vma=False
    )
```
